512 devices in a mesh: wide: 32 (over x, z), narrow: 16 (over y, core).
Axes of the slice: x: 4, y: 8, z: 8, core: 2. Of those that a mesh axis runs over, the one named last changes fastest.
Arguments:
- tokens: bfloat16 [1024, 256, 512], P(('wide', 'narrow')), may hold values from -6 to 6
- cotangent: bfloat16 [1024, 256, 512], P(('wide', 'narrow')), may hold values from -0.29882812 to 0.29882812
- lengths: int32 [1024], P(('wide', 'narrow')), may hold values from 160 to 256, as said below
- item_rows: int32 [1024, 256], P(('wide', 'narrow')), may hold values from 0 to 16383, as said below
- w_in: bfloat16 [512, 2048], replicated, may hold values from -0.25 to 0.25
- w_out: bfloat16 [512, 512], replicated, may hold values from -0.25 to 0.25
- table: float32 [16384, 512], P(('wide', 'narrow')), may hold values from -6 to 6
- moment_one: float32 [16384, 512], P(('wide', 'narrow')), may hold values from -0.3 to 0.3
- moment_two: float32 [16384, 512], P(('wide', 'narrow')), may hold values from 0.0001 to 0.01
Outputs:
- table_new: float32 [16384, 512], P(('wide', 'narrow'))
- moment_one_new: float32 [16384, 512], P(('wide', 'narrow'))
- moment_two_new: float32 [16384, 512], P(('wide', 'narrow'))
The draws below stay inside these ranges and needn't reach their ends.
Inputs may be any that keep to these rules, and one draw needn't show every extreme that they name: `lengths`: some sequence has exactly 256 live positions. `item_rows`: A row r has inner block index (r // 32) % 16. In every sequence at most 32 of the 256 positions name rows of one inner block index, and some index is named by exactly 32 of them.
All inputs are finite; a program needn't handle non-finite values.
Results may differ from the reference program's by a relative error of at most 0.005.
Values may be sent and summed in bfloat16 or wider, within the bound.
A program may use at most 64 MiB of HBM per device.

```python
import math
import jax
import jax.numpy as jnp
from jax import lax

D = 512
HEADS = 8
MICRO = 2
LMAX = 256
ROWS_DEV = 32
SEQS = 1024
ITEMS = 16384
CAP = 32
N_WIDE = 32
N_NARROW = 16


def draw_lengths(key, part):
    first_key, second_key = jax.random.split(jax.random.fold_in(key, 11))
    heavy_low = jax.random.randint(first_key, (SEQS,), 13 * LMAX // 16, LMAX + 1)
    light_low = jax.random.randint(jax.random.fold_in(first_key, 5), (SEQS,), 5 * LMAX // 8, 13 * LMAX // 16)
    wide_index = jnp.arange(SEQS) // (MICRO * N_NARROW)
    values = jnp.where(wide_index < N_WIDE // 2, heavy_low, light_low)
    chosen = jax.random.randint(second_key, (), 0, SEQS)
    return jnp.where(jnp.arange(SEQS) == chosen, LMAX, values).astype(jnp.int32)


def draw_item_rows(key, part):
    base_key = jax.random.fold_in(key, 23)
    owned = N_WIDE * ROWS_DEV
    order_keys = jax.random.split(jax.random.fold_in(base_key, 1), N_NARROW)
    orders = jax.vmap(lambda order_key: jax.random.permutation(order_key, owned))(order_keys)
    sequence_keys = jax.random.split(jax.random.fold_in(base_key, 2), SEQS)

    def one_sequence(seq_key):
        key_full, key_other, key_place, key_left, key_right = jax.random.split(seq_key, 5)
        full_owner = jax.random.randint(key_full, (), 0, N_NARROW)
        others = jax.random.permutation(key_other, (N_NARROW - 1) * CAP)[:LMAX - CAP]
        other_owner = (full_owner + 1 + others // CAP) % N_NARROW
        owner_all = jnp.concatenate([jnp.full((CAP,), full_owner, jnp.int32), other_owner.astype(jnp.int32)])
        owner_seq = owner_all[jax.random.permutation(key_place, LMAX)]
        left_draw = jax.random.randint(key_left, (LMAX,), 0, owned)
        right_draw = jax.random.randint(key_right, (LMAX,), 0, owned)
        skewed = left_draw * right_draw // owned
        local_row = orders[owner_seq, skewed]
        outer_block = local_row // ROWS_DEV
        within = local_row % ROWS_DEV
        return ((outer_block * N_NARROW + owner_seq) * ROWS_DEV + within).astype(jnp.int32)
    return jax.vmap(one_sequence)(sequence_keys)


def block_levels(own_key, dims, cuts, low, high):
    factor_of, own = 1.0, jax.random.fold_in(own_key, 6)
    for dim, parts in cuts:
        draws = jnp.exp(jax.random.uniform(jax.random.fold_in(own, dim), (parts,), jnp.float32, low / len(cuts), high / len(cuts)))
        factor_of = factor_of * jnp.repeat(draws, dims[dim] // parts).reshape([-1 if axis == dim else 1 for axis in range(len(dims))])
    return factor_of


def scatter_about(key, shape, spread, most, cuts=(), dtype=jnp.bfloat16):
    level = block_levels(key, shape, cuts, -0.22, 0.18) if cuts else 1.0
    array = jax.random.normal(key, shape, jnp.float32) * spread * level
    return jnp.minimum(jnp.maximum(array, -most), most).astype(dtype)


def setup_inputs(seed: int = 0) -> dict:
    key_list = jax.random.split(jax.random.key(seed), 10)
    return {
        "tokens": scatter_about(key_list[0], (SEQS, LMAX, D), 1.0, 6.0, ((0, 512),)),
        "cotangent": scatter_about(key_list[1], (SEQS, LMAX, D), 0.05, 0.29882812, ((0, 512),)),
        "lengths": draw_lengths(jax.random.fold_in(key_list[9], 71), 0),
        "item_rows": draw_item_rows(jax.random.fold_in(key_list[9], 71), 0),
        "w_in": scatter_about(key_list[4], (D, 4 * D), D ** -0.5, 0.25),
        "w_out": scatter_about(key_list[5], (D, D), D ** -0.5, 0.25),
        "table": scatter_about(key_list[6], (ITEMS, D), 1.0, 6.0, ((0, 512),), jnp.float32),
        "moment_one": scatter_about(key_list[7], (ITEMS, D), 0.05, 0.3, ((0, 512),), jnp.float32),
        "moment_two": jnp.clip(jnp.exp(math.log(0.01) - 4.6051702 * jax.random.uniform(key_list[8], (ITEMS, D), jnp.float32) ** block_levels(key_list[8], (ITEMS, D), ((0, 512),), -0.2, 0.2)), 0.0001, 0.01),
    }


norm_eps = 1e-06
clip_norm = 4.0
learn_rate = 0.5
beta_first = 0.9
beta_second = 0.999
adam_step = 3.0
adam_eps = 1e-08

def layer_forward(source, w_in, w_out, length):
    positions, width = source.shape
    per_head = width // HEADS
    inner = jnp.dot(source.astype(jnp.bfloat16), w_in, preferred_element_type=jnp.float32)
    hidden = jax.nn.silu(inner).astype(jnp.bfloat16)
    gate_part, value_part, query_part, key_part = jnp.split(hidden, 4, axis=1)
    query_part = query_part.reshape(positions, HEADS, per_head).astype(jnp.float32)
    key_part = key_part.reshape(positions, HEADS, per_head).astype(jnp.float32)
    value_part = value_part.reshape(positions, HEADS, per_head).astype(jnp.float32)
    scores = jnp.einsum('qhd,khd->hqk', query_part, key_part) * per_head ** (-0.5)
    index_row = jnp.arange(positions)
    allowed = ((index_row[None, :] <= index_row[:, None]) & (index_row[:, None] < length)).astype(jnp.float32)
    attention = (jax.nn.silu(scores) * allowed[None] / length.astype(jnp.float32)).astype(jnp.bfloat16)
    mixed = jnp.einsum('hqk,khd->qhd', attention.astype(jnp.float32), value_part).reshape(positions, width)
    centered = mixed - lax.optimization_barrier(jnp.mean(mixed, axis=1, keepdims=True))
    normed = centered * lax.rsqrt(lax.optimization_barrier(jnp.mean(centered * centered, axis=1, keepdims=True)) + norm_eps)
    gated = (normed * gate_part.astype(jnp.float32)).astype(jnp.bfloat16)
    return jnp.dot(gated, w_out, preferred_element_type=jnp.float32) + source

def token_grads(inputs, cotangent, length, w_in, w_out):
    live_mask = (jnp.arange(inputs.shape[0]) < length).astype(jnp.float32)
    _, pullback = jax.vjp(lambda source_rows: layer_forward(source_rows, w_in, w_out, length), inputs.astype(jnp.float32))
    gradient, = pullback(cotangent.astype(jnp.float32) * live_mask[:, None])
    return gradient.astype(jnp.bfloat16)

def adam_rows(row_grad, table, moment_one, moment_two):
    row_norms = jnp.sqrt(lax.optimization_barrier(jnp.sum(row_grad * row_grad, axis=1, keepdims=True)))
    clipped = row_grad * (clip_norm / jnp.maximum(row_norms, clip_norm))
    first_moment = beta_first * moment_one + (1.0 - beta_first) * clipped
    second_moment = beta_second * moment_two + (1.0 - beta_second) * clipped * clipped
    step_size = learn_rate / (1.0 - beta_first ** adam_step)
    scaled = jnp.sqrt(second_moment / (1.0 - beta_second ** adam_step)) + adam_eps
    return (table - step_size * first_moment / scaled, first_moment, second_moment)

def reference(tokens, cotangent, lengths, item_rows, w_in, w_out, table, moment_one, moment_two):
    gradients = lax.map(lambda pieces: token_grads(pieces[0], pieces[1], pieces[2], w_in, w_out), (tokens, cotangent, lengths))
    flat_rows = gradients.reshape(-1, gradients.shape[-1]).astype(jnp.float32)
    row_grad = jax.ops.segment_sum(flat_rows, item_rows.reshape(-1).astype(jnp.int32), num_segments=ITEMS)
    return adam_rows(row_grad, table, moment_one, moment_two)
```

```python
import functools

import jax
import jax.numpy as jnp
from jax import lax
from jax.experimental import pallas as pl
from jax.experimental.pallas import tpu as pltpu
from jax.sharding import PartitionSpec as P

HEADS = 8
BF = jnp.bfloat16
F32 = jnp.float32
I32 = jnp.int32
MESH = pl.DeviceIdType.MESH
CW = 128
X_CHIPS = 4

norm_eps = 1e-06
clip_norm = 4.0
learn_rate = 0.5
beta_first = 0.9
beta_second = 0.999
adam_step = 3.0
adam_eps = 1e-08


def nn(a, b):
    return lax.dot_general(a, b, (((1,), (0,)), ((), ())), preferred_element_type=F32)


def nt(a, b):
    return lax.dot_general(a, b, (((1,), (1,)), ((), ())), preferred_element_type=F32)


def adam_rows(row_grad, table, moment_one, moment_two):
    row_norms = jnp.sqrt(jnp.sum(row_grad * row_grad, axis=1, keepdims=True))
    clipped = row_grad * (clip_norm / jnp.maximum(row_norms, clip_norm))
    first_moment = beta_first * moment_one + (1.0 - beta_first) * clipped
    second_moment = beta_second * moment_two + (1.0 - beta_second) * clipped * clipped
    step_size = learn_rate / (1.0 - beta_first**adam_step)
    scaled = jnp.sqrt(second_moment / (1.0 - beta_second**adam_step)) + adam_eps
    return (table - step_size * first_moment / scaled, first_moment, second_moment)


def iota(shape, dim):
    return lax.broadcasted_iota(I32, shape, dim)


def as_one(flags):
    return jnp.where(flags, 1.0, 0.0).astype(BF)


def layout_rows(s, items, owners, cap, rows_dev, pack, lab_send):
    positions = items.shape[1]
    ids = items[pl.ds(s, 1), :]
    ids_col = jnp.transpose(jnp.broadcast_to(ids.astype(F32), (8, positions)))[:, 0:1].astype(I32)
    owner = (ids // rows_dev) % owners
    owner_col = (ids_col // rows_dev) % owners
    before = (owner_col == owner) & (iota((positions, positions), 0) < iota((positions, positions), 1))
    rank = jnp.sum(jnp.where(before, 1.0, 0.0), axis=0, keepdims=True)
    rank_col = jnp.transpose(jnp.broadcast_to(rank, (8, positions)))[:, 0:1].astype(I32)
    slot = owner * cap + rank.astype(I32)
    pack[s] = as_one(iota((owners * cap, positions), 0) == slot)
    ranks = as_one(iota((positions, 128), 1) % cap == rank_col)
    mine = iota((owners, positions), 0) == owner
    high = jnp.where(mine, (ids // (rows_dev * owners) + 1).astype(F32), 0.0).astype(BF)
    low = jnp.where(mine, (ids % rows_dev).astype(F32), 0.0).astype(BF)
    labels = (nn(high, ranks) - 1.0) * float(rows_dev) + nn(low, ranks)
    for d in range(owners):
        lab_send[d, pl.ds(s, 1), :] = labels[d : d + 1, :]


def sequence_grad(s, tokens, cot, lengths, w_in, w_out, hid, der, att, fac, mixed, ds, dmx, dinner, wmask):
    positions, width = tokens.shape[1:]
    half = positions // 2
    per_head = width // HEADS
    x = tokens[s]
    n = lengths[s]
    for part in range(4):
        cols = slice(part * width, (part + 1) * width)
        inner = nn(x, w_in[:, cols])
        sig = 0.5 * jnp.tanh(0.5 * inner) + 0.5
        act = inner * sig
        hid[:, cols] = act.astype(BF)
        der[:, cols] = sig + act * (1.0 - sig)
    pos = iota((positions, 1), 0)
    live = jnp.where(pos < n, 1.0, 0.0)
    weight = live / jnp.full((positions, 1), n, I32).astype(F32)
    causal = iota((half, half), 1) <= iota((half, half), 0)
    wmask[0] = jnp.where(causal, weight[:half], 0.0)
    wmask[1] = jnp.broadcast_to(weight[half:], (half, half))
    wmask[2] = jnp.where(causal, weight[half:], 0.0)
    low = iota((positions, 128), 1) < per_head
    ones = (jnp.where(iota((1, 128), 1) < per_head, 1.0, 0.0).astype(BF), jnp.where(iota((1, 128), 1) < per_head, 0.0, 1.0).astype(BF))
    scale = per_head ** (-0.5)

    def score(block, wm):
        sig = 0.5 * jnp.tanh(0.5 * block) + 0.5
        act = block * sig
        return (act * wm).astype(BF), (sig + act * (1.0 - sig)) * wm

    for pair in range(HEADS // 2):
        v2 = hid[:, width + pair * 128 : width + (pair + 1) * 128]
        q2 = hid[:, 2 * width + pair * 128 : 2 * width + (pair + 1) * 128]
        k2 = hid[:, 3 * width + pair * 128 : 3 * width + (pair + 1) * 128]
        for h in range(2):
            head = 2 * pair + h
            qm = q2 * (ones[h] * scale)
            a, f = score(nt(qm[:half], k2[:half]), wmask[0])
            att[head, :half, :half] = a
            fac[head, :half, :half] = f
            below = nt(qm[half:], k2)
            a, f = score(below[:, :half], wmask[1])
            att[head, half:, :half] = a
            fac[head, half:, :half] = f
            a, f = score(below[:, half:], wmask[2])
            att[head, half:, half:] = a
            fac[head, half:, half:] = f
        mixed[:, pair * 128 : (pair + 1) * 128] = jnp.where(low, nn(att[2 * pair], v2), nn(att[2 * pair + 1], v2))

    mix = mixed[...]
    centered = mix - jnp.mean(mix, axis=1, keepdims=True)
    inv = lax.rsqrt(jnp.mean(centered * centered, axis=1, keepdims=True) + norm_eps)
    normed = centered * inv
    dgated = (nt(cot[s], w_out[...]) * live).astype(BF).astype(F32)
    gate = hid[:, :width].astype(F32)
    dgate = (dgated * normed).astype(BF).astype(F32)
    dinner[:, :width] = (dgate * der[:, :width]).astype(BF)
    dnormed = dgated * gate
    dcentered = inv * (dnormed - normed * jnp.mean(dnormed * normed, axis=1, keepdims=True))
    dmx[...] = (dcentered - jnp.mean(dcentered, axis=1, keepdims=True)).astype(BF)

    for pair in range(HEADS // 2):
        lanes = slice(pair * 128, (pair + 1) * 128)
        v_at = slice(width + pair * 128, width + (pair + 1) * 128)
        q_at = slice(2 * width + pair * 128, 2 * width + (pair + 1) * 128)
        k_at = slice(3 * width + pair * 128, 3 * width + (pair + 1) * 128)
        v2, k2 = hid[:, v_at], hid[:, k_at]
        dm2 = dmx[:, lanes]
        dm2_t = jnp.transpose(dm2)
        q2_t = jnp.transpose(hid[:, q_at])
        for h in range(2):
            head = 2 * pair + h
            dmm = dm2 * ones[h]
            d = nt(dmm[:half], v2[:half])
            ds[h, :half, :half] = (d.astype(BF).astype(F32) * fac[head, :half, :half]).astype(BF)
            d = nt(dmm[half:], v2)
            ds[h, half:, :] = (d.astype(BF).astype(F32) * fac[head, half:, :]).astype(BF)
        dv = jnp.concatenate([nn(dm2_t[:per_head], att[2 * pair]), nn(dm2_t[per_head:], att[2 * pair + 1])], axis=0)
        dk = jnp.concatenate([nn(q2_t[:per_head], ds[0]), nn(q2_t[per_head:], ds[1])], axis=0)
        dq = jnp.where(low, nn(ds[0], k2), nn(ds[1], k2))
        dinner[:, v_at] = (jnp.transpose(dv).astype(BF).astype(F32) * der[:, v_at]).astype(BF)
        dinner[:, q_at] = ((dq * scale).astype(BF).astype(F32) * der[:, q_at]).astype(BF)
        dinner[:, k_at] = ((jnp.transpose(dk) * scale).astype(BF).astype(F32) * der[:, k_at]).astype(BF)
    return live


def kernel(
    dims, tokens, cot, lengths, items, w_in, w_out, out,
    hid, der, att, fac, mixed, ds, dmx, dinner, wmask, pack, lab_send, lab_recv, onehot,
    send_y, recv_y, acc, send_x, recv_x, own_z, send_z, recv_z,
    sem_lab, sem_y_send, sem_y_recv, sem_x_send, sem_x_recv, sem_z_send, sem_z_recv,
):
    nx, nz, ny, cores, rows_dev = dims
    micro, positions, width = tokens.shape
    owners = ny * cores
    cap = 2 * positions // owners
    slots = owners * cap
    owned = nx * nz * rows_dev
    x_rows = nz * rows_dev
    chunks = width // CW
    wide, narrow = lax.axis_index("wide"), lax.axis_index("narrow")
    my_x, my_z = wide // nz, wide % nz
    my_y, my_core = narrow // cores, narrow % cores

    hops = sorted(((dy, dc) for dy in range(ny) for dc in range(cores)), key=lambda h: (-min(h[0], ny - h[0]), h[1], h[0]))
    hops.remove((0, 0))
    near = [((my_y + dy) % ny) * cores + (my_core + dc) % cores for dy, dc in hops]
    x_peers = [(my_x + d) % nx for d in range(1, nx)]
    z_peers = [(my_z + d) % nz for d in range(1, nz)]

    barrier = pltpu.get_barrier_semaphore()
    for peer in near:
        pl.semaphore_signal(barrier, inc=1, device_id=(wide, peer), device_id_type=MESH)
    for peer in x_peers:
        pl.semaphore_signal(barrier, inc=1, device_id=(peer * nz + my_z, narrow), device_id_type=MESH)
    for peer in z_peers:
        pl.semaphore_signal(barrier, inc=1, device_id=(my_x * nz + peer, narrow), device_id_type=MESH)

    half = positions // 2
    for head in range(HEADS):
        att[head, :half, half:] = jnp.zeros((half, half), BF)
    for h in range(2):
        ds[h, :half, half:] = jnp.zeros((half, half), BF)

    lab_send[...] = jnp.zeros(lab_send.shape, F32)
    for s in range(micro):
        layout_rows(s, items, owners, cap, rows_dev, pack, lab_send)
    lab_recv[0] = lab_send[narrow]

    def one_sequence(s, carry):
        live = sequence_grad(s, tokens, cot, lengths, w_in, w_out, hid, der, att, fac, mixed, ds, dmx, dinner, wmask)

        @pl.when(s == 0)
        def _():
            pl.semaphore_wait(barrier, len(near) + len(x_peers) + len(z_peers))
            for k, peer in enumerate(near):
                pltpu.make_async_remote_copy(
                    lab_send.at[peer], lab_recv.at[k + 1], sem_lab.at[0], sem_lab.at[1],
                    device_id=(wide, peer), device_id_type=MESH,
                ).start()

        for w in range(width // 256):
            cols = slice(w * 256, (w + 1) * 256)
            dx = nt(dinner[...], w_in[cols, :]).astype(BF).astype(F32)
            grad = (dx + cot[s, :, cols].astype(F32) * live).astype(BF)
            packed = nn(pack[s], grad).astype(BF)
            for c in range(w * 256 // CW, (w + 1) * 256 // CW):
                send_y[s, c] = packed[:, c * CW - w * 256 : (c + 1) * CW - w * 256]
                for k, peer in enumerate(near):
                    pltpu.make_async_remote_copy(
                        send_y.at[s, c, pl.ds(pl.multiple_of(peer * cap, cap), cap)],
                        recv_y.at[s, c, pl.ds((k + 1) * cap, cap)],
                        sem_y_send.at[s, c], sem_y_recv.at[s, c],
                        device_id=(wide, peer), device_id_type=MESH,
                    ).start()
                recv_y[s, c, :cap] = send_y[s, c, pl.ds(pl.multiple_of(narrow * cap, cap), cap), :]
        return carry

    lax.fori_loop(0, micro, one_sequence, 0)

    def whole(src, dst, send, recv):
        return pltpu.make_async_remote_copy(src, dst, send, recv, device_id=(wide, narrow), device_id_type=MESH)

    labels_in = whole(lab_send.at[pl.ds(1, owners - 1)], lab_recv.at[pl.ds(1, owners - 1)], sem_lab.at[0], sem_lab.at[1])
    labels_in.wait_recv()
    group = 128 // cap
    lane = iota((1, 128), 1)
    for s in range(micro):
        for g in range(slots // 128):
            row = lab_recv[g * group, s : s + 1, :]
            for k in range(1, group):
                row = jnp.where(lane >= k * cap, lab_recv[g * group + k, s : s + 1, :], row)
            onehot[s, :, g * 128 : (g + 1) * 128] = as_one(iota((owned, 128), 0) == row.astype(I32))

    def y_copy(s, c):
        return whole(send_y.at[s, c, pl.ds(cap, slots - cap)], recv_y.at[s, c, pl.ds(cap, slots - cap)], sem_y_send.at[s, c], sem_y_recv.at[s, c])

    def x_copy(c, d):
        peer = x_peers[d]
        return pltpu.make_async_remote_copy(
            send_x.at[c, pl.ds(pl.multiple_of(peer * x_rows, x_rows), x_rows)], recv_x.at[c, d],
            sem_x_send.at[c, d], sem_x_recv.at[c, d],
            device_id=(peer * nz + my_z, narrow), device_id_type=MESH,
        )

    def z_copy(c, d):
        peer = z_peers[d]
        return pltpu.make_async_remote_copy(
            send_z.at[c, pl.ds(pl.multiple_of(peer * rows_dev, rows_dev), rows_dev)], recv_z.at[c, d],
            sem_z_send.at[c, d], sem_z_recv.at[c, d],
            device_id=(my_x * nz + peer, narrow), device_id_type=MESH,
        )

    def owner_sum(c):
        y_copy(micro - 1, c).wait_recv()
        acc[c] += nn(onehot[micro - 1], recv_y[micro - 1, c])
        send_x[c] = acc[c].astype(BF)
        for d in range(nx - 1):
            x_copy(c, d).start()

    def x_sum(c):
        total = acc[c, pl.ds(pl.multiple_of(my_x * x_rows, x_rows), x_rows), :]
        for d in range(nx - 1):
            x_copy(c, d).wait_recv()
            total += recv_x[c, d].astype(F32)
        own_z[c] = total
        send_z[c] = total.astype(BF)
        for d in range(nz - 1):
            z_copy(c, d).start()

    def z_sum(c):
        total = own_z[c, pl.ds(pl.multiple_of(my_z * rows_dev, rows_dev), rows_dev), :]
        for d in range(nz - 1):
            z_copy(c, d).wait_recv()
            total += recv_z[c, d].astype(F32)
        out[:, c * CW : (c + 1) * CW] = total

    for c in range(chunks):
        for s in range(micro - 1):
            y_copy(s, c).wait_recv()
            part = nn(onehot[s], recv_y[s, c])
            acc[c] = part if s == 0 else acc[c] + part
    for c in range(chunks):
        owner_sum(c)
        if c >= 1:
            x_sum(c - 1)
    x_sum(chunks - 1)
    for c in range(chunks):
        z_sum(c)
    labels_in.wait_send()
    for c in range(chunks):
        for s in range(micro):
            y_copy(s, c).wait_send()
        for d in range(nx - 1):
            x_copy(c, d).wait_send()
        for d in range(nz - 1):
            z_copy(c, d).wait_send()


def on_device(dims, tokens, cotangent, lengths, item_rows, w_in, w_out, table, moment_one, moment_two):
    nx, nz, ny, cores, rows_dev = dims
    micro, positions, width = tokens.shape
    owners = ny * cores
    cap = 2 * positions // owners
    slots = owners * cap
    owned = nx * nz * rows_dev
    x_rows = nz * rows_dev
    chunks = width // CW
    vmem = pl.BlockSpec(memory_space=pltpu.VMEM)
    dma = pltpu.SemaphoreType.DMA
    row_grad = pl.pallas_call(
        functools.partial(kernel, dims),
        out_shape=jax.ShapeDtypeStruct((rows_dev, width), F32),
        in_specs=[vmem, vmem, pl.BlockSpec(memory_space=pltpu.SMEM), vmem, vmem, vmem],
        out_specs=vmem,
        scratch_shapes=[
            pltpu.VMEM((positions, 4 * width), BF),
            pltpu.VMEM((positions, 4 * width), F32),
            pltpu.VMEM((HEADS, positions, positions), BF),
            pltpu.VMEM((HEADS, positions, positions), F32),
            pltpu.VMEM((positions, width), F32),
            pltpu.VMEM((2, positions, positions), BF),
            pltpu.VMEM((positions, width), BF),
            pltpu.VMEM((positions, 4 * width), BF),
            pltpu.VMEM((3, positions // 2, positions // 2), F32),
            pltpu.VMEM((micro, slots, positions), BF),
            pltpu.VMEM((owners, 8, 128), F32),
            pltpu.VMEM((owners, 8, 128), F32),
            pltpu.VMEM((micro, owned, slots), BF),
            pltpu.VMEM((micro, chunks, slots, CW), BF),
            pltpu.VMEM((micro, chunks, slots, CW), BF),
            pltpu.VMEM((chunks, owned, CW), F32),
            pltpu.VMEM((chunks, owned, CW), BF),
            pltpu.VMEM((chunks, nx - 1, x_rows, CW), BF),
            pltpu.VMEM((chunks, x_rows, CW), F32),
            pltpu.VMEM((chunks, x_rows, CW), BF),
            pltpu.VMEM((chunks, nz - 1, rows_dev, CW), BF),
            dma((2,)),
            dma((micro, chunks)),
            dma((micro, chunks)),
            dma((chunks, nx - 1)),
            dma((chunks, nx - 1)),
            dma((chunks, nz - 1)),
            dma((chunks, nz - 1)),
        ],
        compiler_params=pltpu.CompilerParams(collective_id=0, has_side_effects=True, vmem_limit_bytes=56 * 1024 * 1024),
        name="layer_rows",
    )(tokens, cotangent, lengths, item_rows, w_in, w_out)
    return adam_rows(row_grad, table, moment_one, moment_two)


def solution(mesh, x_chips=X_CHIPS, cores=2, rows_dev=32):
    nx = x_chips
    nz = mesh.shape["wide"] // nx
    ny = mesh.shape["narrow"] // cores
    split = P(("wide", "narrow"))
    rows = P(("wide", "narrow"), None)
    return jax.shard_map(
        functools.partial(on_device, (nx, nz, ny, cores, rows_dev)),
        mesh=mesh,
        in_specs=(P(("wide", "narrow"), None, None), P(("wide", "narrow"), None, None), split, rows, P(), P(), rows, rows, rows),
        out_specs=(rows, rows, rows),
        check_vma=False,
    )
```

```python
import functools

import jax
import jax.numpy as jnp
from jax import lax
from jax.experimental import pallas as pl
from jax.experimental.pallas import tpu as pltpu
from jax.sharding import PartitionSpec as P

HEADS = 8
BF = jnp.bfloat16
F32 = jnp.float32
I32 = jnp.int32
MESH = pl.DeviceIdType.MESH
CW = 128
X_CHIPS = 4

norm_eps = 1e-06
clip_norm = 4.0
learn_rate = 0.5
beta_first = 0.9
beta_second = 0.999
adam_step = 3.0
adam_eps = 1e-08


def nn(a, b):
    return lax.dot_general(a, b, (((1,), (0,)), ((), ())), preferred_element_type=F32)


def nt(a, b):
    return lax.dot_general(a, b, (((1,), (1,)), ((), ())), preferred_element_type=F32)


def bits(n):
    return n.bit_length() - 1


def adam_rows(clipped, table, moment_one, moment_two):
    first_moment = beta_first * moment_one + (1.0 - beta_first) * clipped
    second_moment = beta_second * moment_two + (1.0 - beta_second) * clipped * clipped
    step_size = learn_rate / (1.0 - beta_first**adam_step)
    scaled = jnp.sqrt(second_moment / (1.0 - beta_second**adam_step)) + adam_eps
    return (table - step_size * first_moment / scaled, first_moment, second_moment)


def iota(shape, dim):
    return lax.broadcasted_iota(I32, shape, dim)


def as_one(flags):
    return jnp.where(flags, 1.0, 0.0).astype(BF)


def layout_rows(s, items, owners, cap, rows_dev, pack, lab_send):
    positions = items.shape[1]
    ids = items[pl.ds(s, 1), :]
    ids_col = jnp.transpose(jnp.broadcast_to(ids.astype(F32), (8, positions)))[:, 0:1].astype(I32)
    owner = (ids >> bits(rows_dev)) & (owners - 1)
    owner_col = (ids_col >> bits(rows_dev)) & (owners - 1)
    before = (owner_col == owner) & (iota((positions, positions), 0) < iota((positions, positions), 1))
    rank = jnp.sum(jnp.where(before, 1.0, 0.0), axis=0, keepdims=True)
    rank_col = jnp.transpose(jnp.broadcast_to(rank, (8, positions)))[:, 0:1].astype(I32)
    slot = owner * cap + rank.astype(I32)
    pack[s] = as_one(iota((owners * cap, positions), 0) == slot)
    ranks = as_one((iota((positions, 128), 1) & (cap - 1)) == rank_col)
    mine = iota((owners, positions), 0) == owner
    high = jnp.where(mine, ((ids >> bits(rows_dev * owners)) + 1).astype(F32), 0.0).astype(BF)
    low = jnp.where(mine, (ids & (rows_dev - 1)).astype(F32), 0.0).astype(BF)
    labels = (nn(high, ranks) - 1.0) * float(rows_dev) + nn(low, ranks)
    for d in range(owners):
        lab_send[d, pl.ds(s, 1), :] = labels[d : d + 1, :]


def sequence_grad(s, tokens, cot, lengths, w_in, w_out, arrived, hid, der, att, fac, mixed, ds, dmx, dinner, wmask):
    positions, width = tokens.shape[1:]
    half = positions // 2
    per_head = width // HEADS
    arrived("tokens", s)
    x = tokens[s]
    n = lengths[s]
    for part in range(4):
        cols = slice(part * width, (part + 1) * width)
        arrived("w_in", s, part)
        inner = nn(x, w_in[:, cols])
        sig = 0.5 * jnp.tanh(0.5 * inner) + 0.5
        act = inner * sig
        hid[:, cols] = act.astype(BF)
        der[:, cols] = sig + act * (1.0 - sig)
    pos = iota((positions, 1), 0)
    live = jnp.where(pos < n, 1.0, 0.0)
    weight = live / jnp.full((positions, 1), n, I32).astype(F32)
    causal = iota((half, half), 1) <= iota((half, half), 0)
    wmask[0] = jnp.where(causal, weight[:half], 0.0)
    wmask[1] = jnp.broadcast_to(weight[half:], (half, half))
    wmask[2] = jnp.where(causal, weight[half:], 0.0)
    low = iota((positions, 128), 1) < per_head
    ones = (jnp.where(iota((1, 128), 1) < per_head, 1.0, 0.0).astype(BF), jnp.where(iota((1, 128), 1) < per_head, 0.0, 1.0).astype(BF))
    scale = per_head ** (-0.5)

    def score(block, wm):
        sig = 0.5 * jnp.tanh(0.5 * block) + 0.5
        act = block * sig
        return (act * wm).astype(BF), (sig + act * (1.0 - sig)) * wm

    for pair in range(HEADS // 2):
        v2 = hid[:, width + pair * 128 : width + (pair + 1) * 128]
        q2 = hid[:, 2 * width + pair * 128 : 2 * width + (pair + 1) * 128]
        k2 = hid[:, 3 * width + pair * 128 : 3 * width + (pair + 1) * 128]
        for h in range(2):
            head = 2 * pair + h
            qm = q2 * (ones[h] * scale)
            a, f = score(nt(qm[:half], k2[:half]), wmask[0])
            att[head, :half, :half] = a
            fac[head, :half, :half] = f
            below = nt(qm[half:], k2)
            a, f = score(below[:, :half], wmask[1])
            att[head, half:, :half] = a
            fac[head, half:, :half] = f
            a, f = score(below[:, half:], wmask[2])
            att[head, half:, half:] = a
            fac[head, half:, half:] = f
        mixed[:, pair * 128 : (pair + 1) * 128] = jnp.where(low, nn(att[2 * pair], v2), nn(att[2 * pair + 1], v2))

    mix = mixed[...]
    centered = mix - jnp.mean(mix, axis=1, keepdims=True)
    inv = lax.rsqrt(jnp.mean(centered * centered, axis=1, keepdims=True) + norm_eps)
    normed = centered * inv
    arrived("cot", s)
    dgated = (nt(cot[s], w_out[...]) * live).astype(BF).astype(F32)
    gate = hid[:, :width].astype(F32)
    dgate = (dgated * normed).astype(BF).astype(F32)
    dinner[:, :width] = (dgate * der[:, :width]).astype(BF)
    dnormed = dgated * gate
    dcentered = inv * (dnormed - normed * jnp.mean(dnormed * normed, axis=1, keepdims=True))
    dmx[...] = (dcentered - jnp.mean(dcentered, axis=1, keepdims=True)).astype(BF)

    for pair in range(HEADS // 2):
        lanes = slice(pair * 128, (pair + 1) * 128)
        v_at = slice(width + pair * 128, width + (pair + 1) * 128)
        q_at = slice(2 * width + pair * 128, 2 * width + (pair + 1) * 128)
        k_at = slice(3 * width + pair * 128, 3 * width + (pair + 1) * 128)
        v2, k2 = hid[:, v_at], hid[:, k_at]
        dm2 = dmx[:, lanes]
        dm2_t = jnp.transpose(dm2)
        q2_t = jnp.transpose(hid[:, q_at])
        for h in range(2):
            head = 2 * pair + h
            dmm = dm2 * ones[h]
            d = nt(dmm[:half], v2[:half])
            ds[h, :half, :half] = (d.astype(BF).astype(F32) * fac[head, :half, :half]).astype(BF)
            d = nt(dmm[half:], v2)
            ds[h, half:, :] = (d.astype(BF).astype(F32) * fac[head, half:, :]).astype(BF)
        dv = jnp.concatenate([nn(dm2_t[:per_head], att[2 * pair]), nn(dm2_t[per_head:], att[2 * pair + 1])], axis=0)
        dk = jnp.concatenate([nn(q2_t[:per_head], ds[0]), nn(q2_t[per_head:], ds[1])], axis=0)
        dq = jnp.where(low, nn(ds[0], k2), nn(ds[1], k2))
        dinner[:, v_at] = (jnp.transpose(dv).astype(BF).astype(F32) * der[:, v_at]).astype(BF)
        dinner[:, q_at] = ((dq * scale).astype(BF).astype(F32) * der[:, q_at]).astype(BF)
        dinner[:, k_at] = ((jnp.transpose(dk) * scale).astype(BF).astype(F32) * der[:, k_at]).astype(BF)
    return live


def kernel(
    dims, tokens_hbm, cot_hbm, lengths, items_hbm, w_in_hbm, w_out_hbm, out,
    tokens, cot, items, w_in, w_out,
    hid, der, att, fac, mixed, ds, dmx, dinner, wmask, pack, lab_send, lab_recv, onehot,
    send_y, recv_y, acc, send_x, recv_x, own_z, send_z, recv_z,
    sem_in, sem_lab, sem_y_send, sem_y_recv, sem_x_send, sem_x_recv, sem_z_send, sem_z_recv,
):
    nx, nz, ny, cores, rows_dev = dims
    micro, positions, width = tokens.shape
    owners = ny * cores
    cap = 2 * positions // owners
    slots = owners * cap
    owned = nx * nz * rows_dev
    x_rows = nz * rows_dev
    chunks = width // CW
    wide, narrow = lax.axis_index("wide"), lax.axis_index("narrow")
    my_x, my_z = wide >> bits(nz), wide & (nz - 1)
    my_y, my_core = narrow >> bits(cores), narrow & (cores - 1)

    copies = {("items",): pltpu.make_async_copy(items_hbm, items, sem_in.at[0])}
    copies["tokens", 0] = pltpu.make_async_copy(tokens_hbm.at[0], tokens.at[0], sem_in.at[1])
    for part in range(4):
        cols = pl.ds(part * width, width)
        copies["w_in", part] = pltpu.make_async_copy(w_in_hbm.at[:, cols], w_in.at[:, cols], sem_in.at[2 + part])
    copies["w_out",] = pltpu.make_async_copy(w_out_hbm, w_out, sem_in.at[6])
    copies["cot", 0] = pltpu.make_async_copy(cot_hbm.at[0], cot.at[0], sem_in.at[7])
    for s in range(1, micro):
        copies["tokens", s] = pltpu.make_async_copy(tokens_hbm.at[s], tokens.at[s], sem_in.at[6 + 2 * s])
        copies["cot", s] = pltpu.make_async_copy(cot_hbm.at[s], cot.at[s], sem_in.at[7 + 2 * s])
    for copy in copies.values():
        copy.start()

    def arrived(name, s, part=0):
        @pl.when(s == 0)
        def _():
            copies[(name, part)].wait()
            if name == "cot":
                copies["w_out",].wait()

        if name != "w_in":
            for later in range(1, micro):
                pl.when(s == later)(copies[name, later].wait)

    hops = sorted(((dy, dc) for dy in range(ny) for dc in range(cores)), key=lambda h: (-min(h[0], ny - h[0]), h[1], h[0]))
    hops.remove((0, 0))
    near = [((my_y + dy) & (ny - 1)) * cores + ((my_core + dc) & (cores - 1)) for dy, dc in hops]
    x_peers = [(my_x + d) & (nx - 1) for d in range(1, nx)]
    z_peers = [(my_z + d) & (nz - 1) for d in range(1, nz)]

    barrier = pltpu.get_barrier_semaphore()
    for peer in near:
        pl.semaphore_signal(barrier, inc=1, device_id=(wide, peer), device_id_type=MESH)
    for peer in x_peers:
        pl.semaphore_signal(barrier, inc=1, device_id=(peer * nz + my_z, narrow), device_id_type=MESH)
    for peer in z_peers:
        pl.semaphore_signal(barrier, inc=1, device_id=(my_x * nz + peer, narrow), device_id_type=MESH)

    half = positions // 2
    for head in range(HEADS):
        att[head, :half, half:] = jnp.zeros((half, half), BF)
    for h in range(2):
        ds[h, :half, half:] = jnp.zeros((half, half), BF)

    lab_send[...] = jnp.zeros(lab_send.shape, F32)
    copies["items",].wait()
    for s in range(micro):
        layout_rows(s, items, owners, cap, rows_dev, pack, lab_send)
    lab_recv[0] = lab_send[narrow]

    def one_sequence(s, carry):
        live = sequence_grad(s, tokens, cot, lengths, w_in, w_out, arrived, hid, der, att, fac, mixed, ds, dmx, dinner, wmask)

        @pl.when(s == 0)
        def _():
            pl.semaphore_wait(barrier, len(near) + len(x_peers) + len(z_peers))
            for k, peer in enumerate(near):
                pltpu.make_async_remote_copy(
                    lab_send.at[peer], lab_recv.at[k + 1], sem_lab.at[0], sem_lab.at[1],
                    device_id=(wide, peer), device_id_type=MESH,
                ).start()

        for w in range(width // 256):
            cols = slice(w * 256, (w + 1) * 256)
            dx = nt(dinner[...], w_in[cols, :]).astype(BF).astype(F32)
            grad = (dx + cot[s, :, cols].astype(F32) * live).astype(BF)
            packed = nn(pack[s], grad).astype(BF)
            for c in range(w * 256 // CW, (w + 1) * 256 // CW):
                send_y[s, c] = packed[:, c * CW - w * 256 : (c + 1) * CW - w * 256]
                for k, peer in enumerate(near):
                    pltpu.make_async_remote_copy(
                        send_y.at[s, c, pl.ds(pl.multiple_of(peer * cap, cap), cap)],
                        recv_y.at[s, c, pl.ds((k + 1) * cap, cap)],
                        sem_y_send.at[s, c], sem_y_recv.at[s, c],
                        device_id=(wide, peer), device_id_type=MESH,
                    ).start()
                recv_y[s, c, :cap] = send_y[s, c, pl.ds(pl.multiple_of(narrow * cap, cap), cap), :]
        return carry

    lax.fori_loop(0, micro, one_sequence, 0)

    def whole(src, dst, send, recv):
        return pltpu.make_async_remote_copy(src, dst, send, recv, device_id=(wide, narrow), device_id_type=MESH)

    labels_in = whole(lab_send.at[pl.ds(1, owners - 1)], lab_recv.at[pl.ds(1, owners - 1)], sem_lab.at[0], sem_lab.at[1])
    labels_in.wait_recv()
    group = 128 // cap
    lane = iota((1, 128), 1)

    def owner_rows(s):
        for g in range(slots // 128):
            row = lab_recv[g * group, s : s + 1, :]
            for k in range(1, group):
                row = jnp.where(lane >= k * cap, lab_recv[g * group + k, s : s + 1, :], row)
            onehot[s, :, g * 128 : (g + 1) * 128] = as_one(iota((owned, 128), 0) == row.astype(I32))

    def y_copy(s, c):
        return whole(send_y.at[s, c, pl.ds(cap, slots - cap)], recv_y.at[s, c, pl.ds(cap, slots - cap)], sem_y_send.at[s, c], sem_y_recv.at[s, c])

    def x_copy(c, d):
        peer = x_peers[d]
        return pltpu.make_async_remote_copy(
            send_x.at[c, pl.ds(pl.multiple_of(peer * x_rows, x_rows), x_rows)], recv_x.at[c, d],
            sem_x_send.at[c, d], sem_x_recv.at[c, d],
            device_id=(peer * nz + my_z, narrow), device_id_type=MESH,
        )

    def z_copy(c, d):
        peer = z_peers[d]
        return pltpu.make_async_remote_copy(
            send_z.at[c, pl.ds(pl.multiple_of(peer * rows_dev, rows_dev), rows_dev)], recv_z.at[c, d],
            sem_z_send.at[c, d], sem_z_recv.at[c, d],
            device_id=(my_x * nz + peer, narrow), device_id_type=MESH,
        )

    def owner_sum(c):
        y_copy(micro - 1, c).wait_recv()
        acc[c] += nn(onehot[micro - 1], recv_y[micro - 1, c])
        send_x[c] = acc[c].astype(BF)
        for d in range(nx - 1):
            x_copy(c, d).start()

    def x_sum(c):
        total = acc[c, pl.ds(pl.multiple_of(my_x * x_rows, x_rows), x_rows), :]
        for d in range(nx - 1):
            x_copy(c, d).wait_recv()
            total += recv_x[c, d].astype(F32)
        own_z[c] = total
        send_z[c] = total.astype(BF)
        for d in range(nz - 1):
            z_copy(c, d).start()

    def z_sum(c):
        total = own_z[c, pl.ds(pl.multiple_of(my_z * rows_dev, rows_dev), rows_dev), :]
        for d in range(nz - 1):
            z_copy(c, d).wait_recv()
            total += recv_z[c, d].astype(F32)
        out[:, c * CW : (c + 1) * CW] = total
        return jnp.sum(total * total, axis=1, keepdims=True)

    for s in range(micro - 1):
        owner_rows(s)
        for c in range(chunks):
            y_copy(s, c).wait_recv()
            part = nn(onehot[s], recv_y[s, c])
            acc[c] = part if s == 0 else acc[c] + part
    owner_rows(micro - 1)
    for c in range(chunks):
        owner_sum(c)
        if c >= 1:
            x_sum(c - 1)
    x_sum(chunks - 1)
    squares = z_sum(0)
    for c in range(1, chunks):
        squares += z_sum(c)
    out[...] = out[...] * (clip_norm / jnp.maximum(jnp.sqrt(squares), clip_norm))
    labels_in.wait_send()
    for c in range(chunks):
        for s in range(micro):
            y_copy(s, c).wait_send()
        for d in range(nx - 1):
            x_copy(c, d).wait_send()
        for d in range(nz - 1):
            z_copy(c, d).wait_send()


def on_device(dims, tokens, cotangent, lengths, item_rows, w_in, w_out, table, moment_one, moment_two):
    nx, nz, ny, cores, rows_dev = dims
    micro, positions, width = tokens.shape
    owners = ny * cores
    cap = 2 * positions // owners
    slots = owners * cap
    owned = nx * nz * rows_dev
    x_rows = nz * rows_dev
    chunks = width // CW
    vmem = pl.BlockSpec(memory_space=pltpu.VMEM)
    hbm = pl.BlockSpec(memory_space=pl.ANY)
    dma = pltpu.SemaphoreType.DMA
    clipped = pl.pallas_call(
        functools.partial(kernel, dims),
        out_shape=jax.ShapeDtypeStruct((rows_dev, width), F32),
        in_specs=[hbm, hbm, pl.BlockSpec(memory_space=pltpu.SMEM), hbm, hbm, hbm],
        out_specs=vmem,
        scratch_shapes=[
            pltpu.VMEM(tokens.shape, BF),
            pltpu.VMEM(cotangent.shape, BF),
            pltpu.VMEM(item_rows.shape, I32),
            pltpu.VMEM(w_in.shape, BF),
            pltpu.VMEM(w_out.shape, BF),
            pltpu.VMEM((positions, 4 * width), BF),
            pltpu.VMEM((positions, 4 * width), F32),
            pltpu.VMEM((HEADS, positions, positions), BF),
            pltpu.VMEM((HEADS, positions, positions), F32),
            pltpu.VMEM((positions, width), F32),
            pltpu.VMEM((2, positions, positions), BF),
            pltpu.VMEM((positions, width), BF),
            pltpu.VMEM((positions, 4 * width), BF),
            pltpu.VMEM((3, positions // 2, positions // 2), F32),
            pltpu.VMEM((micro, slots, positions), BF),
            pltpu.VMEM((owners, 8, 128), F32),
            pltpu.VMEM((owners, 8, 128), F32),
            pltpu.VMEM((micro, owned, slots), BF),
            pltpu.VMEM((micro, chunks, slots, CW), BF),
            pltpu.VMEM((micro, chunks, slots, CW), BF),
            pltpu.VMEM((chunks, owned, CW), F32),
            pltpu.VMEM((chunks, owned, CW), BF),
            pltpu.VMEM((chunks, nx - 1, x_rows, CW), BF),
            pltpu.VMEM((chunks, x_rows, CW), F32),
            pltpu.VMEM((chunks, x_rows, CW), BF),
            pltpu.VMEM((chunks, nz - 1, rows_dev, CW), BF),
            dma((6 + 2 * micro,)),
            dma((2,)),
            dma((micro, chunks)),
            dma((micro, chunks)),
            dma((chunks, nx - 1)),
            dma((chunks, nx - 1)),
            dma((chunks, nz - 1)),
            dma((chunks, nz - 1)),
        ],
        compiler_params=pltpu.CompilerParams(collective_id=0, has_side_effects=True, vmem_limit_bytes=56 * 1024 * 1024),
        name="layer_rows",
    )(tokens, cotangent, lengths, item_rows, w_in, w_out)
    return adam_rows(clipped, table, moment_one, moment_two)


def solution(mesh, x_chips=X_CHIPS, cores=2, rows_dev=32):
    nx = x_chips
    nz = mesh.shape["wide"] // nx
    ny = mesh.shape["narrow"] // cores
    split = P(("wide", "narrow"))
    rows = P(("wide", "narrow"), None)
    return jax.shard_map(
        functools.partial(on_device, (nx, nz, ny, cores, rows_dev)),
        mesh=mesh,
        in_specs=(P(("wide", "narrow"), None, None), P(("wide", "narrow"), None, None), split, rows, P(), P(), rows, rows, rows),
        out_specs=(rows, rows, rows),
        check_vma=False,
    )
```

```python
import functools

import jax
import jax.numpy as jnp
from jax import lax
from jax.experimental import pallas as pl
from jax.experimental.pallas import tpu as pltpu
from jax.sharding import PartitionSpec as P

HEADS = 8
BF = jnp.bfloat16
F32 = jnp.float32
I32 = jnp.int32
MESH = pl.DeviceIdType.MESH
CW = 128
X_CHIPS = 4

norm_eps = 1e-06
clip_norm = 4.0
learn_rate = 0.5
beta_first = 0.9
beta_second = 0.999
adam_step = 3.0
adam_eps = 1e-08


def nn(a, b):
    return lax.dot_general(a, b, (((1,), (0,)), ((), ())), preferred_element_type=F32)


def nt(a, b):
    return lax.dot_general(a, b, (((1,), (1,)), ((), ())), preferred_element_type=F32)


def bits(n):
    return n.bit_length() - 1


def adam_rows(clipped, table, moment_one, moment_two):
    first_moment = beta_first * moment_one + (1.0 - beta_first) * clipped
    second_moment = beta_second * moment_two + (1.0 - beta_second) * clipped * clipped
    step_size = learn_rate / (1.0 - beta_first**adam_step)
    scaled = jnp.sqrt(second_moment / (1.0 - beta_second**adam_step)) + adam_eps
    return (table - step_size * first_moment / scaled, first_moment, second_moment)


def iota(shape, dim):
    return lax.broadcasted_iota(I32, shape, dim)


def as_one(flags):
    return jnp.where(flags, 1.0, 0.0).astype(BF)


def layout_rows(s, items, owners, cap, rows_dev, pack, lab_send):
    positions = items.shape[1]
    ids = items[pl.ds(s, 1), :]
    ids_col = jnp.transpose(jnp.broadcast_to(ids.astype(F32), (8, positions)))[:, 0:1].astype(I32)
    owner = (ids >> bits(rows_dev)) & (owners - 1)
    owner_col = (ids_col >> bits(rows_dev)) & (owners - 1)
    before = (owner_col == owner) & (iota((positions, positions), 0) < iota((positions, positions), 1))
    rank = jnp.sum(jnp.where(before, 1.0, 0.0), axis=0, keepdims=True)
    rank_col = jnp.transpose(jnp.broadcast_to(rank, (8, positions)))[:, 0:1].astype(I32)
    slot = owner * cap + rank.astype(I32)
    pack[s] = as_one(iota((owners * cap, positions), 0) == slot)
    ranks = as_one((iota((positions, 128), 1) & (cap - 1)) == rank_col)
    mine = iota((owners, positions), 0) == owner
    high = jnp.where(mine, ((ids >> bits(rows_dev * owners)) + 1).astype(F32), 0.0).astype(BF)
    low = jnp.where(mine, (ids & (rows_dev - 1)).astype(F32), 0.0).astype(BF)
    labels = (nn(high, ranks) - 1.0) * float(rows_dev) + nn(low, ranks)
    for d in range(owners):
        lab_send[d, pl.ds(s, 1), :] = labels[d : d + 1, :]


def sequence_grad(s, tokens, cot, lengths, w_in, w_out, arrived, hid, der, att, fac, mixed, ds, dmx, dinner, wmask):
    positions, width = tokens.shape[1:]
    half = positions // 2
    per_head = width // HEADS
    arrived("tokens", s)
    x = tokens[s]
    n = lengths[s]
    for part in range(4):
        cols = slice(part * width, (part + 1) * width)
        arrived("w_in", s, part)
        inner = nn(x, w_in[:, cols])
        sig = 0.5 * jnp.tanh(0.5 * inner) + 0.5
        act = inner * sig
        hid[:, cols] = act.astype(BF)
        der[:, cols] = sig + act * (1.0 - sig)
    pos = iota((positions, 1), 0)
    live = jnp.where(pos < n, 1.0, 0.0)
    weight = live / jnp.full((positions, 1), n, I32).astype(F32)
    causal = iota((half, half), 1) <= iota((half, half), 0)
    wmask[0] = jnp.where(causal, weight[:half], 0.0)
    wmask[1] = jnp.broadcast_to(weight[half:], (half, half))
    wmask[2] = jnp.where(causal, weight[half:], 0.0)
    low = iota((positions, 128), 1) < per_head
    ones = (jnp.where(iota((1, 128), 1) < per_head, 1.0, 0.0).astype(BF), jnp.where(iota((1, 128), 1) < per_head, 0.0, 1.0).astype(BF))
    scale = per_head ** (-0.5)

    def score(block, wm):
        sig = 0.5 * jnp.tanh(0.5 * block) + 0.5
        act = block * sig
        return (act * wm).astype(BF), (sig + act * (1.0 - sig)) * wm

    for pair in range(HEADS // 2):
        v2 = hid[:, width + pair * 128 : width + (pair + 1) * 128]
        q2 = hid[:, 2 * width + pair * 128 : 2 * width + (pair + 1) * 128]
        k2 = hid[:, 3 * width + pair * 128 : 3 * width + (pair + 1) * 128]
        for h in range(2):
            head = 2 * pair + h
            qm = q2 * (ones[h] * scale)
            a, f = score(nt(qm[:half], k2[:half]), wmask[0])
            att[head, :half, :half] = a
            fac[head, :half, :half] = f
            below = nt(qm[half:], k2)
            a, f = score(below[:, :half], wmask[1])
            att[head, half:, :half] = a
            fac[head, half:, :half] = f
            a, f = score(below[:, half:], wmask[2])
            att[head, half:, half:] = a
            fac[head, half:, half:] = f
        mixed[:, pair * 128 : (pair + 1) * 128] = jnp.where(low, nn(att[2 * pair], v2), nn(att[2 * pair + 1], v2))

    mix = mixed[...]
    centered = mix - jnp.mean(mix, axis=1, keepdims=True)
    inv = lax.rsqrt(jnp.mean(centered * centered, axis=1, keepdims=True) + norm_eps)
    normed = centered * inv
    arrived("cot", s)
    dgated = (nt(cot[s], w_out[...]) * live).astype(BF).astype(F32)
    gate = hid[:, :width].astype(F32)
    dgate = (dgated * normed).astype(BF).astype(F32)
    dinner[:, :width] = (dgate * der[:, :width]).astype(BF)
    dnormed = dgated * gate
    dcentered = inv * (dnormed - normed * jnp.mean(dnormed * normed, axis=1, keepdims=True))
    dmx[...] = (dcentered - jnp.mean(dcentered, axis=1, keepdims=True)).astype(BF)

    for pair in range(HEADS // 2):
        lanes = slice(pair * 128, (pair + 1) * 128)
        v_at = slice(width + pair * 128, width + (pair + 1) * 128)
        q_at = slice(2 * width + pair * 128, 2 * width + (pair + 1) * 128)
        k_at = slice(3 * width + pair * 128, 3 * width + (pair + 1) * 128)
        v2, k2 = hid[:, v_at], hid[:, k_at]
        dm2 = dmx[:, lanes]
        dm2_t = jnp.transpose(dm2)
        q2_t = jnp.transpose(hid[:, q_at])
        for h in range(2):
            head = 2 * pair + h
            dmm = dm2 * ones[h]
            d = nt(dmm[:half], v2[:half])
            ds[h, :half, :half] = (d.astype(BF).astype(F32) * fac[head, :half, :half]).astype(BF)
            d = nt(dmm[half:], v2)
            ds[h, half:, :] = (d.astype(BF).astype(F32) * fac[head, half:, :]).astype(BF)
        dv = jnp.concatenate([nn(dm2_t[:per_head], att[2 * pair]), nn(dm2_t[per_head:], att[2 * pair + 1])], axis=0)
        dk = jnp.concatenate([nn(q2_t[:per_head], ds[0]), nn(q2_t[per_head:], ds[1])], axis=0)
        dq = jnp.where(low, nn(ds[0], k2), nn(ds[1], k2))
        dinner[:, v_at] = (jnp.transpose(dv).astype(BF).astype(F32) * der[:, v_at]).astype(BF)
        dinner[:, q_at] = ((dq * scale).astype(BF).astype(F32) * der[:, q_at]).astype(BF)
        dinner[:, k_at] = ((jnp.transpose(dk) * scale).astype(BF).astype(F32) * der[:, k_at]).astype(BF)
    return live


def kernel(
    dims, tokens_hbm, cot_hbm, lengths, items_hbm, w_in_hbm, w_out_hbm, out,
    tokens, cot, items, w_in, w_out,
    hid, der, att, fac, mixed, ds, dmx, dinner, wmask, pack, lab_send, lab_recv, lab_near, onehot, onehot_near, recv_near,
    send_y, recv_y, acc, send_x, recv_x, own_z, send_z, recv_z, send_far, recv_far,
    sem_in, sem_lab, sem_near, sem_far, sem_y_send, sem_y_recv, sem_x_send, sem_x_recv, sem_z_send, sem_z_recv,
):
    nx, nz, ny, cores, rows_dev = dims
    micro, positions, width = tokens.shape
    owners = ny * cores
    cap = 2 * positions // owners
    slots = owners * cap
    owned = nx * nz * rows_dev
    x_rows = nz * rows_dev
    chunks = width // CW
    wide, narrow = lax.axis_index("wide"), lax.axis_index("narrow")
    my_x, my_z = wide >> bits(nz), wide & (nz - 1)
    my_y, my_core = narrow >> bits(cores), narrow & (cores - 1)

    copies = {("items",): pltpu.make_async_copy(items_hbm, items, sem_in.at[0])}
    copies["tokens", 0] = pltpu.make_async_copy(tokens_hbm.at[0], tokens.at[0], sem_in.at[1])
    for part in range(4):
        cols = pl.ds(part * width, width)
        copies["w_in", part] = pltpu.make_async_copy(w_in_hbm.at[:, cols], w_in.at[:, cols], sem_in.at[2 + part])
    copies["w_out",] = pltpu.make_async_copy(w_out_hbm, w_out, sem_in.at[6])
    copies["cot", 0] = pltpu.make_async_copy(cot_hbm.at[0], cot.at[0], sem_in.at[7])
    for s in range(1, micro):
        copies["tokens", s] = pltpu.make_async_copy(tokens_hbm.at[s], tokens.at[s], sem_in.at[6 + 2 * s])
        copies["cot", s] = pltpu.make_async_copy(cot_hbm.at[s], cot.at[s], sem_in.at[7 + 2 * s])
    for copy in copies.values():
        copy.start()

    def arrived(name, s, part=0):
        @pl.when(s == 0)
        def _():
            copies[(name, part)].wait()
            if name == "cot":
                copies["w_out",].wait()

        if name != "w_in":
            for later in range(1, micro):
                pl.when(s == later)(copies[name, later].wait)

    hops = sorted(((dy, dc) for dy in range(ny) for dc in range(cores)), key=lambda h: (-min(h[0], ny - h[0]), h[1], h[0]))
    hops.remove((0, 0))
    near = [((my_y + dy) & (ny - 1)) * cores + ((my_core + dc) & (cores - 1)) for dy, dc in hops]
    quarter = ny // 4
    ahead = [0] + [sign * d for d in range(1, quarter) for sign in (1, -1)]
    if quarter:
        ahead.append(quarter - 2 * quarter * my_core)
    close = [((my_y + dy) & (ny - 1)) * cores + ((my_core + dc) & (cores - 1)) for dy in ahead for dc in range(cores)]

    def opposite(owner):
        return (owner + owners // 2) & (owners - 1)

    x_peers = [(my_x + d) & (nx - 1) for d in range(1, nx)]
    z_peers = [(my_z + d) & (nz - 1) for d in range(1, nz)]

    barrier = pltpu.get_barrier_semaphore()
    for peer in near:
        pl.semaphore_signal(barrier, inc=1, device_id=(wide, peer), device_id_type=MESH)
    for peer in x_peers:
        pl.semaphore_signal(barrier, inc=1, device_id=(peer * nz + my_z, narrow), device_id_type=MESH)
    for peer in z_peers:
        pl.semaphore_signal(barrier, inc=1, device_id=(my_x * nz + peer, narrow), device_id_type=MESH)

    half = positions // 2
    for head in range(HEADS):
        att[head, :half, half:] = jnp.zeros((half, half), BF)
    for h in range(2):
        ds[h, :half, half:] = jnp.zeros((half, half), BF)

    copies["items",].wait()
    for s in range(micro):
        layout_rows(s, items, owners, cap, rows_dev, pack, lab_send)
    lab_recv[0] = lab_send[narrow]
    lab_near[0, 0] = lab_send[narrow]
    lab_near[1, 0] = lab_send[opposite(narrow)]

    def slots_of(owner):
        return pl.ds(pl.multiple_of(owner * cap, cap), cap)

    def send_rows(s, c):
        for k, peer in enumerate(near):
            pltpu.make_async_remote_copy(
                send_y.at[s, c, slots_of(peer)], recv_y.at[s, c, pl.ds((k + 1) * cap, cap)],
                sem_y_send.at[s, c], sem_y_recv.at[s, c],
                device_id=(wide, peer), device_id_type=MESH,
            ).start()
        recv_y[s, c, :cap] = send_y[s, c, slots_of(narrow), :]

    def send_rows_near(s):
        for k, peer in enumerate(close):
            for g, owner in enumerate((peer, opposite(peer))):
                if k == 0:
                    recv_near[s, g, :cap] = send_y[s, 0, slots_of(owner), :]
                else:
                    pltpu.make_async_remote_copy(
                        send_y.at[s, 0, slots_of(owner)], recv_near.at[s, g, pl.ds(k * cap, cap)],
                        sem_near.at[0, s, g], sem_near.at[1, s, g],
                        device_id=(wide, peer), device_id_type=MESH,
                    ).start()

    def one_sequence(s, carry):
        live = sequence_grad(s, tokens, cot, lengths, w_in, w_out, arrived, hid, der, att, fac, mixed, ds, dmx, dinner, wmask)

        @pl.when(s == 0)
        def _():
            pl.semaphore_wait(barrier, len(near) + len(x_peers) + len(z_peers))
            for k, peer in enumerate(near):
                pltpu.make_async_remote_copy(
                    lab_send.at[peer], lab_recv.at[k + 1], sem_lab.at[0], sem_lab.at[1],
                    device_id=(wide, peer), device_id_type=MESH,
                ).start()
            for k, peer in enumerate(close[1:], 1):
                for g, owner in enumerate((peer, opposite(peer))):
                    pltpu.make_async_remote_copy(
                        lab_send.at[owner], lab_near.at[g, k], sem_lab.at[2], sem_lab.at[3],
                        device_id=(wide, peer), device_id_type=MESH,
                    ).start()

        for w in range(width // 256):
            cols = slice(w * 256, (w + 1) * 256)
            dx = nt(dinner[...], w_in[cols, :]).astype(BF).astype(F32)
            grad = (dx + cot[s, :, cols].astype(F32) * live).astype(BF)
            packed = nn(pack[s], grad).astype(BF)
            for c in range(w * 256 // CW, (w + 1) * 256 // CW):
                send_y[s, c] = packed[:, c * CW - w * 256 : (c + 1) * CW - w * 256]
                if c == 0:
                    send_rows_near(s)
                    for earlier in range(micro - 1):
                        pl.when(s == earlier + 1)(functools.partial(send_rows, earlier, chunks - 1))
                elif c < chunks - 1:
                    send_rows(s, c)
                else:
                    pl.when(s == micro - 1)(functools.partial(send_rows, micro - 1, c))
        return carry

    lax.fori_loop(0, micro, one_sequence, 0)

    def whole(src, dst, send, recv):
        return pltpu.make_async_remote_copy(src, dst, send, recv, device_id=(wide, narrow), device_id_type=MESH)

    labels_in = whole(lab_send.at[pl.ds(1, owners - 1)], lab_recv.at[pl.ds(1, owners - 1)], sem_lab.at[0], sem_lab.at[1])
    near_count = 2 * (owners // 2 - 1)
    labels_near = whole(lab_send.at[pl.ds(1, near_count)], lab_recv.at[pl.ds(1, near_count)], sem_lab.at[2], sem_lab.at[3])
    labels_near.wait_recv()
    labels_in.wait_recv()
    group = 128 // cap
    lane = iota((1, 128), 1)

    def owner_rows(s, count, labels):
        blocks = []
        for g in range(count // 128):
            row = labels[g * group, s : s + 1, :]
            for k in range(1, group):
                row = jnp.where(lane >= k * cap, labels[g * group + k, s : s + 1, :], row)
            blocks.append(as_one(iota((owned, 128), 0) == row.astype(I32)))
        return blocks

    def near_copy(s, g):
        rest = pl.ds(cap, slots // 2 - cap)
        return whole(send_y.at[s, 0, rest], recv_near.at[s, g, rest], sem_near.at[0, s, g], sem_near.at[1, s, g])

    def y_copy(s, c):
        return whole(send_y.at[s, c, pl.ds(cap, slots - cap)], recv_y.at[s, c, pl.ds(cap, slots - cap)], sem_y_send.at[s, c], sem_y_recv.at[s, c])

    def x_copy(c, d):
        peer = x_peers[d]
        return pltpu.make_async_remote_copy(
            send_x.at[c, pl.ds(pl.multiple_of(peer * x_rows, x_rows), x_rows)], recv_x.at[c, d],
            sem_x_send.at[c, d], sem_x_recv.at[c, d],
            device_id=(peer * nz + my_z, narrow), device_id_type=MESH,
        )

    def z_copy(c, d):
        peer = z_peers[d]
        return pltpu.make_async_remote_copy(
            send_z.at[c, pl.ds(pl.multiple_of(peer * rows_dev, rows_dev), rows_dev)], recv_z.at[c, d],
            sem_z_send.at[c, d], sem_z_recv.at[c, d],
            device_id=(my_x * nz + peer, narrow), device_id_type=MESH,
        )

    def x_send(c):
        send_x[c] = acc[c].astype(BF)
        for d in range(nx - 1):
            x_copy(c, d).start()

    def owner_sum(c):
        y_copy(micro - 1, c).wait_recv()
        acc[c] += nn(onehot[micro - 1], recv_y[micro - 1, c])
        x_send(c)

    def x_sum(c):
        total = acc[c, pl.ds(pl.multiple_of(my_x * x_rows, x_rows), x_rows), :]
        for d in range(nx - 1):
            x_copy(c, d).wait_recv()
            total += recv_x[c, d].astype(F32)
        own_z[c] = total
        send_z[c] = total.astype(BF)
        for d in range(nz - 1):
            z_copy(c, d).start()

    def z_sum(c):
        total = own_z[c, pl.ds(pl.multiple_of(my_z * rows_dev, rows_dev), rows_dev), :]
        for d in range(nz - 1):
            z_copy(c, d).wait_recv()
            total += recv_z[c, d].astype(F32)
        return total

    def far_copy():
        return pltpu.make_async_remote_copy(
            send_far, recv_far, sem_far.at[0], sem_far.at[1],
            device_id=(wide, opposite(narrow)), device_id_type=MESH,
        )

    def finish(c, total):
        out[:, c * CW : (c + 1) * CW] = total
        return jnp.sum(total * total, axis=1, keepdims=True)

    for s in range(micro):
        for g in range(2):
            for i, block in enumerate(owner_rows(s, slots // 2, lab_near.at[g])):
                onehot_near[s, g, :, i * 128 : (i + 1) * 128] = block
    far = chunks
    for s in range(micro):
        for g, c in enumerate((0, far)):
            near_copy(s, g).wait_recv()
            part = nn(onehot_near[s, g], recv_near[s, g])
            acc[c] = part if s == 0 else acc[c] + part
            if s == micro - 1:
                x_send(c)
    for s in range(micro):
        for i, block in enumerate(owner_rows(s, slots, lab_recv)):
            onehot[s, :, i * 128 : (i + 1) * 128] = block
    for s in range(micro - 1):
        for c in range(1, chunks):
            y_copy(s, c).wait_recv()
            part = nn(onehot[s], recv_y[s, c])
            acc[c] = part if s == 0 else acc[c] + part
    x_sum(0)
    owner_sum(1)
    x_sum(far)
    for c in range(2, chunks):
        owner_sum(c)
        x_sum(c - 1)
    send_far[...] = z_sum(far).astype(BF)
    far_copy().start()
    x_sum(chunks - 1)
    squares = 0.0
    for c in range(1, chunks - 1):
        squares += finish(c, z_sum(c))
    total = z_sum(0)
    far_copy().wait_recv()
    squares += finish(0, total + recv_far[...].astype(F32))
    squares += finish(chunks - 1, z_sum(chunks - 1))
    out[...] = out[...] * (clip_norm / jnp.maximum(jnp.sqrt(squares), clip_norm))
    labels_in.wait_send()
    labels_near.wait_send()
    far_copy().wait_send()
    for s in range(micro):
        for g in range(2):
            near_copy(s, g).wait_send()
        for c in range(1, chunks):
            y_copy(s, c).wait_send()
    for c in range(chunks + 1):
        for d in range(nx - 1):
            x_copy(c, d).wait_send()
        for d in range(nz - 1):
            z_copy(c, d).wait_send()


def on_device(dims, tokens, cotangent, lengths, item_rows, w_in, w_out, table, moment_one, moment_two):
    nx, nz, ny, cores, rows_dev = dims
    micro, positions, width = tokens.shape
    owners = ny * cores
    cap = 2 * positions // owners
    slots = owners * cap
    owned = nx * nz * rows_dev
    x_rows = nz * rows_dev
    chunks = width // CW
    vmem = pl.BlockSpec(memory_space=pltpu.VMEM)
    hbm = pl.BlockSpec(memory_space=pl.ANY)
    dma = pltpu.SemaphoreType.DMA
    clipped = pl.pallas_call(
        functools.partial(kernel, dims),
        out_shape=jax.ShapeDtypeStruct((rows_dev, width), F32),
        in_specs=[hbm, hbm, pl.BlockSpec(memory_space=pltpu.SMEM), hbm, hbm, hbm],
        out_specs=vmem,
        scratch_shapes=[
            pltpu.VMEM(tokens.shape, BF),
            pltpu.VMEM(cotangent.shape, BF),
            pltpu.VMEM(item_rows.shape, I32),
            pltpu.VMEM(w_in.shape, BF),
            pltpu.VMEM(w_out.shape, BF),
            pltpu.VMEM((positions, 4 * width), BF),
            pltpu.VMEM((positions, 4 * width), F32),
            pltpu.VMEM((HEADS, positions, positions), BF),
            pltpu.VMEM((HEADS, positions, positions), F32),
            pltpu.VMEM((positions, width), F32),
            pltpu.VMEM((2, positions, positions), BF),
            pltpu.VMEM((positions, width), BF),
            pltpu.VMEM((positions, 4 * width), BF),
            pltpu.VMEM((3, positions // 2, positions // 2), F32),
            pltpu.VMEM((micro, slots, positions), BF),
            pltpu.VMEM((owners, micro, 128), F32),
            pltpu.VMEM((owners, micro, 128), F32),
            pltpu.VMEM((2, owners // 2, micro, 128), F32),
            pltpu.VMEM((micro, owned, slots), BF),
            pltpu.VMEM((micro, 2, owned, slots // 2), BF),
            pltpu.VMEM((micro, 2, slots // 2, CW), BF),
            pltpu.VMEM((micro, chunks, slots, CW), BF),
            pltpu.VMEM((micro, chunks, slots, CW), BF),
            pltpu.VMEM((chunks + 1, owned, CW), F32),
            pltpu.VMEM((chunks + 1, owned, CW), BF),
            pltpu.VMEM((chunks + 1, max(nx - 1, 1), x_rows, CW), BF),
            pltpu.VMEM((chunks + 1, x_rows, CW), F32),
            pltpu.VMEM((chunks + 1, x_rows, CW), BF),
            pltpu.VMEM((chunks + 1, max(nz - 1, 1), rows_dev, CW), BF),
            pltpu.VMEM((rows_dev, CW), BF),
            pltpu.VMEM((rows_dev, CW), BF),
            dma((6 + 2 * micro,)),
            dma((4,)),
            dma((2, micro, 2)),
            dma((2,)),
            dma((micro, chunks)),
            dma((micro, chunks)),
            dma((chunks + 1, max(nx - 1, 1))),
            dma((chunks + 1, max(nx - 1, 1))),
            dma((chunks + 1, max(nz - 1, 1))),
            dma((chunks + 1, max(nz - 1, 1))),
        ],
        compiler_params=pltpu.CompilerParams(collective_id=0, has_side_effects=True, vmem_limit_bytes=56 * 1024 * 1024),
        name="layer_rows",
    )(tokens, cotangent, lengths, item_rows, w_in, w_out)
    return adam_rows(clipped, table, moment_one, moment_two)


def solution(mesh, x_chips=X_CHIPS, cores=2, rows_dev=32):
    nx = x_chips
    nz = mesh.shape["wide"] // nx
    ny = mesh.shape["narrow"] // cores
    split = P(("wide", "narrow"))
    rows = P(("wide", "narrow"), None)
    return jax.shard_map(
        functools.partial(on_device, (nx, nz, ny, cores, rows_dev)),
        mesh=mesh,
        in_specs=(P(("wide", "narrow"), None, None), P(("wide", "narrow"), None, None), split, rows, P(), P(), rows, rows, rows),
        out_specs=(rows, rows, rows),
        check_vma=False,
    )
```

```python
import functools

import jax
import jax.numpy as jnp
from jax import lax
from jax.experimental import pallas as pl
from jax.experimental.pallas import tpu as pltpu
from jax.sharding import PartitionSpec as P

HEADS = 8
BF = jnp.bfloat16
F32 = jnp.float32
I32 = jnp.int32
MESH = pl.DeviceIdType.MESH
CW = 128
SHORT = 2
X_CHIPS = 4

norm_eps = 1e-06
clip_norm = 4.0
learn_rate = 0.5
beta_first = 0.9
beta_second = 0.999
adam_step = 3.0
adam_eps = 1e-08


def nn(a, b):
    return lax.dot_general(a, b, (((1,), (0,)), ((), ())), preferred_element_type=F32)


def nt(a, b):
    return lax.dot_general(a, b, (((1,), (1,)), ((), ())), preferred_element_type=F32)


def bits(n):
    return n.bit_length() - 1


def adam_rows(clipped, table, moment_one, moment_two):
    first_moment = beta_first * moment_one + (1.0 - beta_first) * clipped
    second_moment = beta_second * moment_two + (1.0 - beta_second) * clipped * clipped
    step_size = learn_rate / (1.0 - beta_first**adam_step)
    scaled = jnp.sqrt(second_moment / (1.0 - beta_second**adam_step)) + adam_eps
    return (table - step_size * first_moment / scaled, first_moment, second_moment)


def iota(shape, dim):
    return lax.broadcasted_iota(I32, shape, dim)


def as_one(flags):
    return jnp.where(flags, 1.0, 0.0).astype(BF)


def layout_rows(s, items, owners, cap, rows_dev, pack, lab_send):
    positions = items.shape[1]
    ids = items[pl.ds(s, 1), :]
    ids_col = jnp.transpose(jnp.broadcast_to(ids.astype(F32), (8, positions)))[:, 0:1].astype(I32)
    owner = (ids >> bits(rows_dev)) & (owners - 1)
    owner_col = (ids_col >> bits(rows_dev)) & (owners - 1)
    before = (owner_col == owner) & (iota((positions, positions), 0) < iota((positions, positions), 1))
    rank = jnp.sum(jnp.where(before, 1.0, 0.0), axis=0, keepdims=True)
    rank_col = jnp.transpose(jnp.broadcast_to(rank, (8, positions)))[:, 0:1].astype(I32)
    slot = owner * cap + rank.astype(I32)
    pack[s] = as_one(iota((owners * cap, positions), 0) == slot)
    ranks = as_one((iota((positions, 128), 1) & (cap - 1)) == rank_col)
    mine = iota((owners, positions), 0) == owner
    high = jnp.where(mine, ((ids >> bits(rows_dev * owners)) + 1).astype(F32), 0.0).astype(BF)
    low = jnp.where(mine, (ids & (rows_dev - 1)).astype(F32), 0.0).astype(BF)
    labels = (nn(high, ranks) - 1.0) * float(rows_dev) + nn(low, ranks)
    for d in range(owners):
        lab_send[d, pl.ds(s, 1), :] = labels[d : d + 1, :]


def sequence_grad(s, tokens, cot, lengths, w_in, w_out, arrived, hid, der, att, fac, mixed, ds, dmx, dinner, wmask):
    positions, width = tokens.shape[1:]
    half = positions // 2
    per_head = width // HEADS
    arrived("tokens", s)
    x = tokens[s]
    n = lengths[s]
    for part in range(4):
        cols = slice(part * width, (part + 1) * width)
        arrived("w_in", s, part)
        inner = nn(x, w_in[:, cols])
        sig = 0.5 * jnp.tanh(0.5 * inner) + 0.5
        act = inner * sig
        hid[:, cols] = act.astype(BF)
        der[:, cols] = sig + act * (1.0 - sig)
    pos = iota((positions, 1), 0)
    live = jnp.where(pos < n, 1.0, 0.0)
    weight = live / jnp.full((positions, 1), n, I32).astype(F32)
    causal = iota((half, half), 1) <= iota((half, half), 0)
    wmask[0] = jnp.where(causal, weight[:half], 0.0)
    wmask[1] = jnp.broadcast_to(weight[half:], (half, half))
    wmask[2] = jnp.where(causal, weight[half:], 0.0)
    low = iota((positions, 128), 1) < per_head
    ones = (jnp.where(iota((1, 128), 1) < per_head, 1.0, 0.0).astype(BF), jnp.where(iota((1, 128), 1) < per_head, 0.0, 1.0).astype(BF))
    scale = per_head ** (-0.5)

    def score(block, wm):
        sig = 0.5 * jnp.tanh(0.5 * block) + 0.5
        act = block * sig
        return (act * wm).astype(BF), (sig + act * (1.0 - sig)) * wm

    for pair in range(HEADS // 2):
        v2 = hid[:, width + pair * 128 : width + (pair + 1) * 128]
        q2 = hid[:, 2 * width + pair * 128 : 2 * width + (pair + 1) * 128]
        k2 = hid[:, 3 * width + pair * 128 : 3 * width + (pair + 1) * 128]
        for h in range(2):
            head = 2 * pair + h
            qm = q2 * (ones[h] * scale)
            a, f = score(nt(qm[:half], k2[:half]), wmask[0])
            att[head, :half, :half] = a
            fac[head, :half, :half] = f
            below = nt(qm[half:], k2)
            a, f = score(below[:, :half], wmask[1])
            att[head, half:, :half] = a
            fac[head, half:, :half] = f
            a, f = score(below[:, half:], wmask[2])
            att[head, half:, half:] = a
            fac[head, half:, half:] = f
        mixed[:, pair * 128 : (pair + 1) * 128] = jnp.where(low, nn(att[2 * pair], v2), nn(att[2 * pair + 1], v2))

    mix = mixed[...]
    centered = mix - jnp.mean(mix, axis=1, keepdims=True)
    inv = lax.rsqrt(jnp.mean(centered * centered, axis=1, keepdims=True) + norm_eps)
    normed = centered * inv
    arrived("cot", s)
    dgated = (nt(cot[s], w_out[...]) * live).astype(BF).astype(F32)
    gate = hid[:, :width].astype(F32)
    dgate = (dgated * normed).astype(BF).astype(F32)
    dinner[:, :width] = (dgate * der[:, :width]).astype(BF)
    dnormed = dgated * gate
    dcentered = inv * (dnormed - normed * jnp.mean(dnormed * normed, axis=1, keepdims=True))
    dmx[...] = (dcentered - jnp.mean(dcentered, axis=1, keepdims=True)).astype(BF)

    for pair in range(HEADS // 2):
        lanes = slice(pair * 128, (pair + 1) * 128)
        v_at = slice(width + pair * 128, width + (pair + 1) * 128)
        q_at = slice(2 * width + pair * 128, 2 * width + (pair + 1) * 128)
        k_at = slice(3 * width + pair * 128, 3 * width + (pair + 1) * 128)
        v2, k2 = hid[:, v_at], hid[:, k_at]
        dm2 = dmx[:, lanes]
        dm2_t = jnp.transpose(dm2)
        q2_t = jnp.transpose(hid[:, q_at])
        for h in range(2):
            head = 2 * pair + h
            dmm = dm2 * ones[h]
            d = nt(dmm[:half], v2[:half])
            ds[h, :half, :half] = (d.astype(BF).astype(F32) * fac[head, :half, :half]).astype(BF)
            d = nt(dmm[half:], v2)
            ds[h, half:, :] = (d.astype(BF).astype(F32) * fac[head, half:, :]).astype(BF)
        dv = jnp.concatenate([nn(dm2_t[:per_head], att[2 * pair]), nn(dm2_t[per_head:], att[2 * pair + 1])], axis=0)
        dk = jnp.concatenate([nn(q2_t[:per_head], ds[0]), nn(q2_t[per_head:], ds[1])], axis=0)
        dq = jnp.where(low, nn(ds[0], k2), nn(ds[1], k2))
        dinner[:, v_at] = (jnp.transpose(dv).astype(BF).astype(F32) * der[:, v_at]).astype(BF)
        dinner[:, q_at] = ((dq * scale).astype(BF).astype(F32) * der[:, q_at]).astype(BF)
        dinner[:, k_at] = ((jnp.transpose(dk) * scale).astype(BF).astype(F32) * der[:, k_at]).astype(BF)
    return live


def kernel(
    dims, tokens_hbm, cot_hbm, lengths, items_hbm, w_in_hbm, w_out_hbm, out,
    tokens, cot, items, w_in, w_out,
    hid, der, att, fac, mixed, ds, dmx, dinner, wmask, pack, lab_send, lab_recv, lab_near, onehot, onehot_near, recv_near,
    send_y, recv_y, acc, send_x, recv_x, own_z, send_z, recv_z, send_zf, recv_zf, own_xf, send_xf, recv_xf, send_far, recv_far,
    sem_in, sem_lab, sem_near, sem_far, sem_zf, sem_xf, sem_sub, sem_y_send, sem_y_recv, sem_x_send, sem_x_recv, sem_z_send, sem_z_recv,
):
    nx, nz, ny, cores, rows_dev = dims
    micro, positions, width = tokens.shape
    owners = ny * cores
    cap = 2 * positions // owners
    slots = owners * cap
    owned = nx * nz * rows_dev
    x_rows = nz * rows_dev
    chunks = width // CW
    wide, narrow = lax.axis_index("wide"), lax.axis_index("narrow")
    my_x, my_z = wide >> bits(nz), wide & (nz - 1)
    my_y, my_core = narrow >> bits(cores), narrow & (cores - 1)

    copies = {("items",): pltpu.make_async_copy(items_hbm, items, sem_in.at[0])}
    copies["tokens", 0] = pltpu.make_async_copy(tokens_hbm.at[0], tokens.at[0], sem_in.at[1])
    for part in range(4):
        cols = pl.ds(part * width, width)
        copies["w_in", part] = pltpu.make_async_copy(w_in_hbm.at[:, cols], w_in.at[:, cols], sem_in.at[2 + part])
    copies["w_out",] = pltpu.make_async_copy(w_out_hbm, w_out, sem_in.at[6])
    copies["cot", 0] = pltpu.make_async_copy(cot_hbm.at[0], cot.at[0], sem_in.at[7])
    for s in range(1, micro):
        copies["tokens", s] = pltpu.make_async_copy(tokens_hbm.at[s], tokens.at[s], sem_in.at[6 + 2 * s])
        copies["cot", s] = pltpu.make_async_copy(cot_hbm.at[s], cot.at[s], sem_in.at[7 + 2 * s])
    for copy in copies.values():
        copy.start()

    def arrived(name, s, part=0):
        @pl.when(s == 0)
        def _():
            copies[(name, part)].wait()
            if name == "cot":
                copies["w_out",].wait()

        if name != "w_in":
            for later in range(1, micro):
                pl.when(s == later)(copies[name, later].wait)

    hops = sorted(((dy, dc) for dy in range(ny) for dc in range(cores)), key=lambda h: (-min(h[0], ny - h[0]), h[1], h[0]))
    hops.remove((0, 0))
    near = [((my_y + dy) & (ny - 1)) * cores + ((my_core + dc) & (cores - 1)) for dy, dc in hops]
    quarter = ny // 4
    ahead = [0] + [sign * d for d in range(1, quarter) for sign in (1, -1)]
    if quarter:
        ahead.append(quarter - 2 * quarter * my_core)
    close = [((my_y + dy) & (ny - 1)) * cores + ((my_core + dc) & (cores - 1)) for dy in ahead for dc in range(cores)]

    def opposite(owner):
        return (owner + owners // 2) & (owners - 1)

    x_peers = [(my_x + d) & (nx - 1) for d in range(1, nx)]
    z_peers = [(my_z + d) & (nz - 1) for d in range(1, nz)]

    barrier = pltpu.get_barrier_semaphore()
    for peer in near:
        pl.semaphore_signal(barrier, inc=1, device_id=(wide, peer), device_id_type=MESH)
    for peer in x_peers:
        pl.semaphore_signal(barrier, inc=1, device_id=(peer * nz + my_z, narrow), device_id_type=MESH)
    for peer in z_peers:
        pl.semaphore_signal(barrier, inc=1, device_id=(my_x * nz + peer, narrow), device_id_type=MESH)

    half = positions // 2
    for head in range(HEADS):
        att[head, :half, half:] = jnp.zeros((half, half), BF)
    for h in range(2):
        ds[h, :half, half:] = jnp.zeros((half, half), BF)

    copies["items",].wait()
    for s in range(micro):
        layout_rows(s, items, owners, cap, rows_dev, pack, lab_send)
    lab_recv[0] = lab_send[narrow]
    lab_near[0, 0] = lab_send[narrow]
    lab_near[1, 0] = lab_send[opposite(narrow)]

    def slots_of(owner):
        return pl.ds(pl.multiple_of(owner * cap, cap), cap)

    def send_rows(s, c):
        for k, peer in enumerate(near):
            pltpu.make_async_remote_copy(
                send_y.at[s, c, slots_of(peer)], recv_y.at[s, c, pl.ds((k + 1) * cap, cap)],
                sem_y_send.at[s, c], sem_y_recv.at[s, c],
                device_id=(wide, peer), device_id_type=MESH,
            ).start()
        recv_y[s, c, :cap] = send_y[s, c, slots_of(narrow), :]

    def send_rows_near(s, c):
        for k, peer in enumerate(close):
            for g, owner in enumerate((peer, opposite(peer))):
                if k == 0:
                    recv_near[s, c, g, :cap] = send_y[s, c, slots_of(owner), :]
                else:
                    pltpu.make_async_remote_copy(
                        send_y.at[s, c, slots_of(owner)], recv_near.at[s, c, g, pl.ds(k * cap, cap)],
                        sem_near.at[0, s, c, g], sem_near.at[1, s, c, g],
                        device_id=(wide, peer), device_id_type=MESH,
                    ).start()

    def one_sequence(s, carry):
        live = sequence_grad(s, tokens, cot, lengths, w_in, w_out, arrived, hid, der, att, fac, mixed, ds, dmx, dinner, wmask)

        @pl.when(s == 0)
        def _():
            pl.semaphore_wait(barrier, len(near) + len(x_peers) + len(z_peers))
            for k, peer in enumerate(near):
                pltpu.make_async_remote_copy(
                    lab_send.at[peer], lab_recv.at[k + 1], sem_lab.at[0], sem_lab.at[1],
                    device_id=(wide, peer), device_id_type=MESH,
                ).start()
            for k, peer in enumerate(close[1:], 1):
                for g, owner in enumerate((peer, opposite(peer))):
                    pltpu.make_async_remote_copy(
                        lab_send.at[owner], lab_near.at[g, k], sem_lab.at[2], sem_lab.at[3],
                        device_id=(wide, peer), device_id_type=MESH,
                    ).start()

        for w in range(width // 256):
            cols = slice(w * 256, (w + 1) * 256)
            dx = nt(dinner[...], w_in[cols, :]).astype(BF).astype(F32)
            grad = (dx + cot[s, :, cols].astype(F32) * live).astype(BF)
            packed = nn(pack[s], grad).astype(BF)
            for c in range(w * 256 // CW, (w + 1) * 256 // CW):
                send_y[s, c] = packed[:, c * CW - w * 256 : (c + 1) * CW - w * 256]
                if c < SHORT:
                    send_rows_near(s, c)
                if c == SHORT - 1:
                    for earlier in range(micro - 1):
                        pl.when(s == earlier + 1)(functools.partial(send_rows, earlier, chunks - 1))
                if SHORT <= c < chunks - 1:
                    send_rows(s, c)
                if c == chunks - 1:
                    pl.when(s == micro - 1)(functools.partial(send_rows, micro - 1, c))
        return carry

    lax.fori_loop(0, micro, one_sequence, 0)

    def whole(src, dst, send, recv):
        return pltpu.make_async_remote_copy(src, dst, send, recv, device_id=(wide, narrow), device_id_type=MESH)

    labels_in = whole(lab_send.at[pl.ds(1, owners - 1)], lab_recv.at[pl.ds(1, owners - 1)], sem_lab.at[0], sem_lab.at[1])
    near_count = 2 * (owners // 2 - 1)
    labels_near = whole(lab_send.at[pl.ds(1, near_count)], lab_recv.at[pl.ds(1, near_count)], sem_lab.at[2], sem_lab.at[3])
    labels_near.wait_recv()
    labels_in.wait_recv()
    group = 128 // cap
    lane = iota((1, 128), 1)

    def owner_rows(s, count, labels):
        blocks = []
        for g in range(count // 128):
            row = labels[g * group, s : s + 1, :]
            for k in range(1, group):
                row = jnp.where(lane >= k * cap, labels[g * group + k, s : s + 1, :], row)
            blocks.append(as_one(iota((owned, 128), 0) == row.astype(I32)))
        return blocks

    def near_copy(s, c, g):
        rest = pl.ds(cap, slots // 2 - cap)
        return whole(send_y.at[s, c, rest], recv_near.at[s, c, g, rest], sem_near.at[0, s, c, g], sem_near.at[1, s, c, g])

    def y_copy(s, c):
        return whole(send_y.at[s, c, pl.ds(cap, slots - cap)], recv_y.at[s, c, pl.ds(cap, slots - cap)], sem_y_send.at[s, c], sem_y_recv.at[s, c])

    def x_copy(c, d):
        peer = x_peers[d]
        return pltpu.make_async_remote_copy(
            send_x.at[c, pl.ds(pl.multiple_of(peer * x_rows, x_rows), x_rows)], recv_x.at[c, d],
            sem_x_send.at[c, d], sem_x_recv.at[c, d],
            device_id=(peer * nz + my_z, narrow), device_id_type=MESH,
        )

    def z_copy(c, d):
        peer = z_peers[d]
        return pltpu.make_async_remote_copy(
            send_z.at[c, pl.ds(pl.multiple_of(peer * rows_dev, rows_dev), rows_dev)], recv_z.at[c, d],
            sem_z_send.at[c, d], sem_z_recv.at[c, d],
            device_id=(my_x * nz + peer, narrow), device_id_type=MESH,
        )

    last = chunks - 1
    parts = min(nz, 4)
    part_rows = x_rows // parts

    def sub_copy(q, d):
        peer = x_peers[d]
        rows = pl.ds(pl.multiple_of(peer * x_rows + q * part_rows, part_rows), part_rows)
        return pltpu.make_async_remote_copy(
            send_x.at[last, rows], recv_x.at[last, d, pl.ds(q * part_rows, part_rows)],
            sem_sub.at[0, q, d], sem_sub.at[1, q, d],
            device_id=(peer * nz + my_z, narrow), device_id_type=MESH,
        )

    def zf_copy(d):
        peer = z_peers[d]
        return pltpu.make_async_remote_copy(
            send_zf.at[:, peer], recv_zf.at[d], sem_zf.at[0, d], sem_zf.at[1, d],
            device_id=(my_x * nz + peer, narrow), device_id_type=MESH,
        )

    def xf_copy(d):
        peer = x_peers[d]
        return pltpu.make_async_remote_copy(
            send_xf.at[peer], recv_xf.at[d], sem_xf.at[0, d], sem_xf.at[1, d],
            device_id=(peer * nz + my_z, narrow), device_id_type=MESH,
        )

    def zf_send(c):
        send_zf[...] = acc[c].astype(BF).reshape(send_zf.shape)
        for d in range(nz - 1):
            zf_copy(d).start()

    def zf_sum(c):
        rows = [acc[c, pl.ds(pl.multiple_of(x * x_rows + my_z * rows_dev, rows_dev), rows_dev), :] for x in range(nx)]
        for d in range(nz - 1):
            zf_copy(d).wait_recv()
        for x in range(nx):
            total = rows[x]
            for d in range(nz - 1):
                total += recv_zf[d, x].astype(F32)
            own_xf[x] = total
            send_xf[x] = total.astype(BF)
        for d in range(nx - 1):
            xf_copy(d).start()

    def xf_sum():
        total = own_xf[my_x]
        for d in range(nx - 1):
            xf_copy(d).wait_recv()
            total += recv_xf[d].astype(F32)
        return total

    def x_send(c):
        send_x[c] = acc[c].astype(BF)
        if c == last:
            for q in range(parts):
                for d in range(nx - 1):
                    sub_copy(q, d).start()
        else:
            for d in range(nx - 1):
                x_copy(c, d).start()

    def sub_sum(q):
        rows = slice(q * part_rows, (q + 1) * part_rows)
        total = acc[last, pl.ds(pl.multiple_of(my_x * x_rows + q * part_rows, part_rows), part_rows), :]
        for d in range(nx - 1):
            sub_copy(q, d).wait_recv()
            total += recv_x[last, d, rows].astype(F32)
        own_z[last, rows] = total
        send_z[last, rows] = total.astype(BF)
        for d in range(nz - 1):
            pl.when((z_peers[d] >> bits(nz // parts)) == q)(z_copy(last, d).start)

    def owner_sum(c):
        y_copy(micro - 1, c).wait_recv()
        acc[c] += nn(onehot[micro - 1], recv_y[micro - 1, c])
        x_send(c)

    def x_sum(c):
        total = acc[c, pl.ds(pl.multiple_of(my_x * x_rows, x_rows), x_rows), :]
        for d in range(nx - 1):
            x_copy(c, d).wait_recv()
            total += recv_x[c, d].astype(F32)
        own_z[c] = total
        send_z[c] = total.astype(BF)
        for d in range(nz - 1):
            z_copy(c, d).start()

    def z_sum(c):
        total = own_z[c, pl.ds(pl.multiple_of(my_z * rows_dev, rows_dev), rows_dev), :]
        for d in range(nz - 1):
            z_copy(c, d).wait_recv()
            total += recv_z[c, d].astype(F32)
        return total

    def far_copy(i):
        return pltpu.make_async_remote_copy(
            send_far.at[i], recv_far.at[i], sem_far.at[0, i], sem_far.at[1, i],
            device_id=(wide, opposite(narrow)), device_id_type=MESH,
        )

    def finish(c, total):
        out[:, c * CW : (c + 1) * CW] = total
        return jnp.sum(total * total, axis=1, keepdims=True)

    for s in range(micro):
        for g in range(2):
            for i, block in enumerate(owner_rows(s, slots // 2, lab_near.at[g])):
                onehot_near[s, g, :, i * 128 : (i + 1) * 128] = block
    for c in range(SHORT):
        for s in range(micro):
            for g, table in enumerate((c, chunks + c)):
                near_copy(s, c, g).wait_recv()
                part = nn(onehot_near[s, g], recv_near[s, c, g])
                acc[table] = part if s == 0 else acc[table] + part
        if c == 0:
            zf_send(chunks)
        else:
            x_send(chunks + c)
        x_send(c)
    for s in range(micro):
        for i, block in enumerate(owner_rows(s, slots, lab_recv)):
            onehot[s, :, i * 128 : (i + 1) * 128] = block
    for s in range(micro - 1):
        for c in range(SHORT, chunks):
            y_copy(s, c).wait_recv()
            part = nn(onehot[s], recv_y[s, c])
            acc[c] = part if s == 0 else acc[c] + part
    x_sum(0)
    owner_sum(2)
    x_sum(chunks + 1)
    x_sum(1)
    zf_sum(chunks)
    owner_sum(3)
    send_far[0] = xf_sum().astype(BF)
    far_copy(0).start()
    x_sum(2)
    send_far[1] = z_sum(chunks + 1).astype(BF)
    far_copy(1).start()
    for q in range(parts):
        sub_sum(q)
    squares = finish(2, z_sum(2))
    for c in range(SHORT):
        total = z_sum(c)
        far_copy(c).wait_recv()
        squares += finish(c, total + recv_far[c].astype(F32))
    squares += finish(last, z_sum(last))
    out[...] = out[...] * (clip_norm / jnp.maximum(jnp.sqrt(squares), clip_norm))
    labels_in.wait_send()
    labels_near.wait_send()
    for s in range(micro):
        for c in range(SHORT):
            for g in range(2):
                near_copy(s, c, g).wait_send()
        for c in range(SHORT, chunks):
            y_copy(s, c).wait_send()
    for c in range(SHORT):
        far_copy(c).wait_send()
    for d in range(nz - 1):
        zf_copy(d).wait_send()
    for d in range(nx - 1):
        xf_copy(d).wait_send()
        for q in range(parts):
            sub_copy(q, d).wait_send()
    for c in (0, 1, 2, 3, chunks + 1):
        if c != last:
            for d in range(nx - 1):
                x_copy(c, d).wait_send()
        for d in range(nz - 1):
            z_copy(c, d).wait_send()


def on_device(dims, tokens, cotangent, lengths, item_rows, w_in, w_out, table, moment_one, moment_two):
    nx, nz, ny, cores, rows_dev = dims
    micro, positions, width = tokens.shape
    owners = ny * cores
    cap = 2 * positions // owners
    slots = owners * cap
    owned = nx * nz * rows_dev
    x_rows = nz * rows_dev
    chunks = width // CW
    vmem = pl.BlockSpec(memory_space=pltpu.VMEM)
    hbm = pl.BlockSpec(memory_space=pl.ANY)
    dma = pltpu.SemaphoreType.DMA
    clipped = pl.pallas_call(
        functools.partial(kernel, dims),
        out_shape=jax.ShapeDtypeStruct((rows_dev, width), F32),
        in_specs=[hbm, hbm, pl.BlockSpec(memory_space=pltpu.SMEM), hbm, hbm, hbm],
        out_specs=vmem,
        scratch_shapes=[
            pltpu.VMEM(tokens.shape, BF),
            pltpu.VMEM(cotangent.shape, BF),
            pltpu.VMEM(item_rows.shape, I32),
            pltpu.VMEM(w_in.shape, BF),
            pltpu.VMEM(w_out.shape, BF),
            pltpu.VMEM((positions, 4 * width), BF),
            pltpu.VMEM((positions, 4 * width), F32),
            pltpu.VMEM((HEADS, positions, positions), BF),
            pltpu.VMEM((HEADS, positions, positions), F32),
            pltpu.VMEM((positions, width), F32),
            pltpu.VMEM((2, positions, positions), BF),
            pltpu.VMEM((positions, width), BF),
            pltpu.VMEM((positions, 4 * width), BF),
            pltpu.VMEM((3, positions // 2, positions // 2), F32),
            pltpu.VMEM((micro, slots, positions), BF),
            pltpu.VMEM((owners, micro, 128), F32),
            pltpu.VMEM((owners, micro, 128), F32),
            pltpu.VMEM((2, owners // 2, micro, 128), F32),
            pltpu.VMEM((micro, owned, slots), BF),
            pltpu.VMEM((micro, 2, owned, slots // 2), BF),
            pltpu.VMEM((micro, SHORT, 2, slots // 2, CW), BF),
            pltpu.VMEM((micro, chunks, slots, CW), BF),
            pltpu.VMEM((micro, chunks, slots, CW), BF),
            pltpu.VMEM((chunks + 2, owned, CW), F32),
            pltpu.VMEM((chunks + 2, owned, CW), BF),
            pltpu.VMEM((chunks + 2, max(nx - 1, 1), x_rows, CW), BF),
            pltpu.VMEM((chunks + 2, x_rows, CW), F32),
            pltpu.VMEM((chunks + 2, x_rows, CW), BF),
            pltpu.VMEM((chunks + 2, max(nz - 1, 1), rows_dev, CW), BF),
            pltpu.VMEM((nx, nz, rows_dev, CW), BF),
            pltpu.VMEM((max(nz - 1, 1), nx, rows_dev, CW), BF),
            pltpu.VMEM((nx, rows_dev, CW), F32),
            pltpu.VMEM((nx, rows_dev, CW), BF),
            pltpu.VMEM((max(nx - 1, 1), rows_dev, CW), BF),
            pltpu.VMEM((2, rows_dev, CW), BF),
            pltpu.VMEM((2, rows_dev, CW), BF),
            dma((6 + 2 * micro,)),
            dma((4,)),
            dma((2, micro, SHORT, 2)),
            dma((2, 2)),
            dma((2, max(nz - 1, 1))),
            dma((2, max(nx - 1, 1))),
            dma((2, min(nz, 4), max(nx - 1, 1))),
            dma((micro, chunks)),
            dma((micro, chunks)),
            dma((chunks + 2, max(nx - 1, 1))),
            dma((chunks + 2, max(nx - 1, 1))),
            dma((chunks + 2, max(nz - 1, 1))),
            dma((chunks + 2, max(nz - 1, 1))),
        ],
        compiler_params=pltpu.CompilerParams(collective_id=0, has_side_effects=True, vmem_limit_bytes=56 * 1024 * 1024),
        name="layer_rows",
    )(tokens, cotangent, lengths, item_rows, w_in, w_out)
    return adam_rows(clipped, table, moment_one, moment_two)


def solution(mesh, x_chips=X_CHIPS, cores=2, rows_dev=32):
    nx = x_chips
    nz = mesh.shape["wide"] // nx
    ny = mesh.shape["narrow"] // cores
    split = P(("wide", "narrow"))
    rows = P(("wide", "narrow"), None)
    return jax.shard_map(
        functools.partial(on_device, (nx, nz, ny, cores, rows_dev)),
        mesh=mesh,
        in_specs=(P(("wide", "narrow"), None, None), P(("wide", "narrow"), None, None), split, rows, P(), P(), rows, rows, rows),
        out_specs=(rows, rows, rows),
        check_vma=False,
    )
```

```python
import functools

import jax
import jax.numpy as jnp
from jax import lax
from jax.experimental import pallas as pl
from jax.experimental.pallas import tpu as pltpu
from jax.sharding import PartitionSpec as P

HEADS = 8
BF = jnp.bfloat16
F32 = jnp.float32
I32 = jnp.int32
MESH = pl.DeviceIdType.MESH
CW = 128
SHORT = 2
X_CHIPS = 4

norm_eps = 1e-06
clip_norm = 4.0
learn_rate = 0.5
beta_first = 0.9
beta_second = 0.999
adam_step = 3.0
adam_eps = 1e-08


def nn(a, b):
    return lax.dot_general(a, b, (((1,), (0,)), ((), ())), preferred_element_type=F32)


def nt(a, b):
    return lax.dot_general(a, b, (((1,), (1,)), ((), ())), preferred_element_type=F32)


def bits(n):
    return n.bit_length() - 1


def adam_rows(clipped, table, moment_one, moment_two):
    first_moment = beta_first * moment_one + (1.0 - beta_first) * clipped
    second_moment = beta_second * moment_two + (1.0 - beta_second) * clipped * clipped
    step_size = learn_rate / (1.0 - beta_first**adam_step)
    scaled = jnp.sqrt(second_moment / (1.0 - beta_second**adam_step)) + adam_eps
    return (table - step_size * first_moment / scaled, first_moment, second_moment)


def iota(shape, dim):
    return lax.broadcasted_iota(I32, shape, dim)


def as_one(flags):
    return jnp.where(flags, 1.0, 0.0).astype(BF)


def layout_rows(s, items, owners, cap, rows_dev, pack, lab_send):
    positions = items.shape[1]
    ids = items[pl.ds(s, 1), :]
    ids_col = jnp.transpose(jnp.broadcast_to(ids.astype(F32), (8, positions)))[:, 0:1].astype(I32)
    owner = (ids >> bits(rows_dev)) & (owners - 1)
    owner_col = (ids_col >> bits(rows_dev)) & (owners - 1)
    before = (owner_col == owner) & (iota((positions, positions), 0) < iota((positions, positions), 1))
    rank = jnp.sum(jnp.where(before, 1.0, 0.0), axis=0, keepdims=True)
    rank_col = jnp.transpose(jnp.broadcast_to(rank, (8, positions)))[:, 0:1].astype(I32)
    slot = owner * cap + rank.astype(I32)
    pack[s] = as_one(iota((owners * cap, positions), 0) == slot)
    ranks = as_one((iota((positions, 128), 1) & (cap - 1)) == rank_col)
    mine = iota((owners, positions), 0) == owner
    high = jnp.where(mine, ((ids >> bits(rows_dev * owners)) + 1).astype(F32), 0.0).astype(BF)
    low = jnp.where(mine, (ids & (rows_dev - 1)).astype(F32), 0.0).astype(BF)
    labels = (nn(high, ranks) - 1.0) * float(rows_dev) + nn(low, ranks)
    for d in range(owners):
        lab_send[d, pl.ds(s, 1), :] = labels[d : d + 1, :]


def sequence_grad(s, tokens, cot, lengths, w_in, w_out, arrived, hid, der, att, fac, mixed, ds, dmx, dinner, wmask):
    positions, width = tokens.shape[1:]
    half = positions // 2
    per_head = width // HEADS
    arrived("tokens", s)
    x = tokens[s]
    n = lengths[s]
    for part in range(4):
        cols = slice(part * width, (part + 1) * width)
        arrived("w_in", s, part)
        inner = nn(x, w_in[:, cols])
        sig = 0.5 * jnp.tanh(0.5 * inner) + 0.5
        act = inner * sig
        hid[:, cols] = act.astype(BF)
        der[:, cols] = sig + act * (1.0 - sig)
    pos = iota((positions, 1), 0)
    live = jnp.where(pos < n, 1.0, 0.0)
    weight = live / jnp.full((positions, 1), n, I32).astype(F32)
    causal = iota((half, half), 1) <= iota((half, half), 0)
    wmask[0] = jnp.where(causal, weight[:half], 0.0)
    wmask[1] = jnp.broadcast_to(weight[half:], (half, half))
    wmask[2] = jnp.where(causal, weight[half:], 0.0)
    low = iota((positions, 128), 1) < per_head
    ones = (jnp.where(iota((1, 128), 1) < per_head, 1.0, 0.0).astype(BF), jnp.where(iota((1, 128), 1) < per_head, 0.0, 1.0).astype(BF))
    scale = per_head ** (-0.5)

    def score(block, wm):
        sig = 0.5 * jnp.tanh(0.5 * block) + 0.5
        act = block * sig
        return (act * wm).astype(BF), (sig + act * (1.0 - sig)) * wm

    for pair in range(HEADS // 2):
        v2 = hid[:, width + pair * 128 : width + (pair + 1) * 128]
        q2 = hid[:, 2 * width + pair * 128 : 2 * width + (pair + 1) * 128]
        k2 = hid[:, 3 * width + pair * 128 : 3 * width + (pair + 1) * 128]
        for h in range(2):
            head = 2 * pair + h
            qm = q2 * (ones[h] * scale)
            a, f = score(nt(qm[:half], k2[:half]), wmask[0])
            att[head, :half, :half] = a
            fac[head, :half, :half] = f
            below = nt(qm[half:], k2)
            a, f = score(below[:, :half], wmask[1])
            att[head, half:, :half] = a
            fac[head, half:, :half] = f
            a, f = score(below[:, half:], wmask[2])
            att[head, half:, half:] = a
            fac[head, half:, half:] = f
        mixed[:, pair * 128 : (pair + 1) * 128] = jnp.where(low, nn(att[2 * pair], v2), nn(att[2 * pair + 1], v2))

    mix = mixed[...]
    centered = mix - jnp.mean(mix, axis=1, keepdims=True)
    inv = lax.rsqrt(jnp.mean(centered * centered, axis=1, keepdims=True) + norm_eps)
    normed = centered * inv
    arrived("cot", s)
    dgated = (nt(cot[s], w_out[...]) * live).astype(BF).astype(F32)
    gate = hid[:, :width].astype(F32)
    dgate = (dgated * normed).astype(BF).astype(F32)
    dinner[:, :width] = (dgate * der[:, :width]).astype(BF)
    dnormed = dgated * gate
    dcentered = inv * (dnormed - normed * jnp.mean(dnormed * normed, axis=1, keepdims=True))
    dmx[...] = (dcentered - jnp.mean(dcentered, axis=1, keepdims=True)).astype(BF)

    for pair in range(HEADS // 2):
        lanes = slice(pair * 128, (pair + 1) * 128)
        v_at = slice(width + pair * 128, width + (pair + 1) * 128)
        q_at = slice(2 * width + pair * 128, 2 * width + (pair + 1) * 128)
        k_at = slice(3 * width + pair * 128, 3 * width + (pair + 1) * 128)
        v2, k2 = hid[:, v_at], hid[:, k_at]
        dm2 = dmx[:, lanes]
        dm2_t = jnp.transpose(dm2)
        q2_t = jnp.transpose(hid[:, q_at])
        for h in range(2):
            head = 2 * pair + h
            dmm = dm2 * ones[h]
            d = nt(dmm[:half], v2[:half])
            ds[h, :half, :half] = (d.astype(BF).astype(F32) * fac[head, :half, :half]).astype(BF)
            d = nt(dmm[half:], v2)
            ds[h, half:, :] = (d.astype(BF).astype(F32) * fac[head, half:, :]).astype(BF)
        dv = jnp.concatenate([nn(dm2_t[:per_head], att[2 * pair]), nn(dm2_t[per_head:], att[2 * pair + 1])], axis=0)
        dk = jnp.concatenate([nn(q2_t[:per_head], ds[0]), nn(q2_t[per_head:], ds[1])], axis=0)
        dq = jnp.where(low, nn(ds[0], k2), nn(ds[1], k2))
        dinner[:, v_at] = (jnp.transpose(dv).astype(BF).astype(F32) * der[:, v_at]).astype(BF)
        dinner[:, q_at] = ((dq * scale).astype(BF).astype(F32) * der[:, q_at]).astype(BF)
        dinner[:, k_at] = ((jnp.transpose(dk) * scale).astype(BF).astype(F32) * der[:, k_at]).astype(BF)
    return live


def kernel(
    dims, tokens_hbm, cot_hbm, lengths, items_hbm, w_in_hbm, w_out_hbm, out,
    tokens, cot, items, w_in, w_out,
    hid, der, att, fac, mixed, ds, dmx, dinner, wmask, pack, lab_send, lab_recv, lab_near, onehot, onehot_near, recv_near,
    send_y, recv_y, acc, send_x, recv_x, own_z, send_z, recv_z, send_zf, recv_zf, own_xf, send_xf, recv_xf, send_far, recv_far,
    sem_in, sem_lab, sem_near, sem_far, sem_zf, sem_xf, sem_sub, sem_y_send, sem_y_recv, sem_x_send, sem_x_recv, sem_z_send, sem_z_recv,
):
    nx, nz, ny, cores, rows_dev = dims
    micro, positions, width = tokens.shape
    owners = ny * cores
    cap = 2 * positions // owners
    slots = owners * cap
    owned = nx * nz * rows_dev
    x_rows = nz * rows_dev
    chunks = width // CW
    wide, narrow = lax.axis_index("wide"), lax.axis_index("narrow")
    my_x, my_z = wide >> bits(nz), wide & (nz - 1)
    my_y, my_core = narrow >> bits(cores), narrow & (cores - 1)

    copies = {("items",): pltpu.make_async_copy(items_hbm, items, sem_in.at[0])}
    copies["tokens", 0] = pltpu.make_async_copy(tokens_hbm.at[0], tokens.at[0], sem_in.at[1])
    for part in range(4):
        cols = pl.ds(part * width, width)
        copies["w_in", part] = pltpu.make_async_copy(w_in_hbm.at[:, cols], w_in.at[:, cols], sem_in.at[2 + part])
    copies["w_out",] = pltpu.make_async_copy(w_out_hbm, w_out, sem_in.at[6])
    copies["cot", 0] = pltpu.make_async_copy(cot_hbm.at[0], cot.at[0], sem_in.at[7])
    for s in range(1, micro):
        copies["tokens", s] = pltpu.make_async_copy(tokens_hbm.at[s], tokens.at[s], sem_in.at[6 + 2 * s])
        copies["cot", s] = pltpu.make_async_copy(cot_hbm.at[s], cot.at[s], sem_in.at[7 + 2 * s])
    for copy in copies.values():
        copy.start()

    def arrived(name, s, part=0):
        @pl.when(s == 0)
        def _():
            copies[(name, part)].wait()
            if name == "cot":
                copies["w_out",].wait()

        if name != "w_in":
            for later in range(1, micro):
                pl.when(s == later)(copies[name, later].wait)

    hops = sorted(((dy, dc) for dy in range(ny) for dc in range(cores)), key=lambda h: (-min(h[0], ny - h[0]), h[1], h[0]))
    hops.remove((0, 0))
    near = [((my_y + dy) & (ny - 1)) * cores + ((my_core + dc) & (cores - 1)) for dy, dc in hops]
    quarter = ny // 4
    ahead = [0] + [sign * d for d in range(1, quarter) for sign in (1, -1)]
    if quarter:
        ahead.append(quarter - 2 * quarter * my_core)
    close = [((my_y + dy) & (ny - 1)) * cores + ((my_core + dc) & (cores - 1)) for dy in ahead for dc in range(cores)]

    def opposite(owner):
        return (owner + owners // 2) & (owners - 1)

    x_peers = [(my_x + d) & (nx - 1) for d in range(1, nx)]
    z_peers = [(my_z + d) & (nz - 1) for d in range(1, nz)]

    barrier = pltpu.get_barrier_semaphore()
    for peer in near:
        pl.semaphore_signal(barrier, inc=1, device_id=(wide, peer), device_id_type=MESH)
    for peer in x_peers:
        pl.semaphore_signal(barrier, inc=1, device_id=(peer * nz + my_z, narrow), device_id_type=MESH)
    for peer in z_peers:
        pl.semaphore_signal(barrier, inc=1, device_id=(my_x * nz + peer, narrow), device_id_type=MESH)

    half = positions // 2
    for head in range(HEADS):
        att[head, :half, half:] = jnp.zeros((half, half), BF)
    for h in range(2):
        ds[h, :half, half:] = jnp.zeros((half, half), BF)

    copies["items",].wait()
    for s in range(micro):
        layout_rows(s, items, owners, cap, rows_dev, pack, lab_send)
    lab_recv[0] = lab_send[narrow]
    lab_near[0, 0] = lab_send[narrow]
    lab_near[1, 0] = lab_send[opposite(narrow)]

    def slots_of(owner):
        return pl.ds(pl.multiple_of(owner * cap, cap), cap)

    def send_rows(s, c):
        for k, peer in enumerate(near):
            pltpu.make_async_remote_copy(
                send_y.at[s, c, slots_of(peer)], recv_y.at[s, c, pl.ds((k + 1) * cap, cap)],
                sem_y_send.at[s, c], sem_y_recv.at[s, c],
                device_id=(wide, peer), device_id_type=MESH,
            ).start()
        recv_y[s, c, :cap] = send_y[s, c, slots_of(narrow), :]

    def send_rows_near(s, c):
        for k, peer in enumerate(close):
            for g, owner in enumerate((peer, opposite(peer))):
                if k == 0:
                    recv_near[s, c, g, :cap] = send_y[s, c, slots_of(owner), :]
                else:
                    pltpu.make_async_remote_copy(
                        send_y.at[s, c, slots_of(owner)], recv_near.at[s, c, g, pl.ds(k * cap, cap)],
                        sem_near.at[0, s, c, g], sem_near.at[1, s, c, g],
                        device_id=(wide, peer), device_id_type=MESH,
                    ).start()

    def one_sequence(s, carry):
        live = sequence_grad(s, tokens, cot, lengths, w_in, w_out, arrived, hid, der, att, fac, mixed, ds, dmx, dinner, wmask)

        @pl.when(s == 0)
        def _():
            pl.semaphore_wait(barrier, len(near) + len(x_peers) + len(z_peers))
            for k, peer in enumerate(near):
                pltpu.make_async_remote_copy(
                    lab_send.at[peer], lab_recv.at[k + 1], sem_lab.at[0], sem_lab.at[1],
                    device_id=(wide, peer), device_id_type=MESH,
                ).start()
            for k, peer in enumerate(close[1:], 1):
                for g, owner in enumerate((peer, opposite(peer))):
                    pltpu.make_async_remote_copy(
                        lab_send.at[owner], lab_near.at[g, k], sem_lab.at[2], sem_lab.at[3],
                        device_id=(wide, peer), device_id_type=MESH,
                    ).start()

        for w in range(width // 256):
            cols = slice(w * 256, (w + 1) * 256)
            dx = nt(dinner[...], w_in[cols, :]).astype(BF).astype(F32)
            grad = (dx + cot[s, :, cols].astype(F32) * live).astype(BF)
            packed = nn(pack[s], grad).astype(BF)
            for c in range(w * 256 // CW, (w + 1) * 256 // CW):
                send_y[s, c] = packed[:, c * CW - w * 256 : (c + 1) * CW - w * 256]
                if c < SHORT:
                    send_rows_near(s, c)
                if c == SHORT:
                    pl.when(s < micro - 1)(functools.partial(send_rows, s, c))
        return carry

    lax.fori_loop(0, micro, one_sequence, 0)
    send_rows(0, chunks - 1)

    def whole(src, dst, send, recv):
        return pltpu.make_async_remote_copy(src, dst, send, recv, device_id=(wide, narrow), device_id_type=MESH)

    labels_in = whole(lab_send.at[pl.ds(1, owners - 1)], lab_recv.at[pl.ds(1, owners - 1)], sem_lab.at[0], sem_lab.at[1])
    near_count = 2 * (owners // 2 - 1)
    labels_near = whole(lab_send.at[pl.ds(1, near_count)], lab_recv.at[pl.ds(1, near_count)], sem_lab.at[2], sem_lab.at[3])
    labels_near.wait_recv()
    labels_in.wait_recv()
    group = 128 // cap
    lane = iota((1, 128), 1)

    def owner_rows(s, count, labels):
        blocks = []
        for g in range(count // 128):
            row = labels[g * group, s : s + 1, :]
            for k in range(1, group):
                row = jnp.where(lane >= k * cap, labels[g * group + k, s : s + 1, :], row)
            blocks.append(as_one(iota((owned, 128), 0) == row.astype(I32)))
        return blocks

    def near_copy(s, c, g):
        rest = pl.ds(cap, slots // 2 - cap)
        return whole(send_y.at[s, c, rest], recv_near.at[s, c, g, rest], sem_near.at[0, s, c, g], sem_near.at[1, s, c, g])

    def y_copy(s, c):
        return whole(send_y.at[s, c, pl.ds(cap, slots - cap)], recv_y.at[s, c, pl.ds(cap, slots - cap)], sem_y_send.at[s, c], sem_y_recv.at[s, c])

    def x_copy(c, d):
        peer = x_peers[d]
        return pltpu.make_async_remote_copy(
            send_x.at[c, pl.ds(pl.multiple_of(peer * x_rows, x_rows), x_rows)], recv_x.at[c, d],
            sem_x_send.at[c, d], sem_x_recv.at[c, d],
            device_id=(peer * nz + my_z, narrow), device_id_type=MESH,
        )

    def z_copy(c, d):
        peer = z_peers[d]
        return pltpu.make_async_remote_copy(
            send_z.at[c, pl.ds(pl.multiple_of(peer * rows_dev, rows_dev), rows_dev)], recv_z.at[c, d],
            sem_z_send.at[c, d], sem_z_recv.at[c, d],
            device_id=(my_x * nz + peer, narrow), device_id_type=MESH,
        )

    last = chunks - 1
    parts = min(nz, 4)
    part_rows = x_rows // parts

    def sub_copy(q, d):
        peer = x_peers[d]
        rows = pl.ds(pl.multiple_of(peer * x_rows + q * part_rows, part_rows), part_rows)
        return pltpu.make_async_remote_copy(
            send_x.at[last, rows], recv_x.at[last, d, pl.ds(q * part_rows, part_rows)],
            sem_sub.at[0, q, d], sem_sub.at[1, q, d],
            device_id=(peer * nz + my_z, narrow), device_id_type=MESH,
        )

    def zf_copy(d):
        peer = z_peers[d]
        return pltpu.make_async_remote_copy(
            send_zf.at[:, peer], recv_zf.at[d], sem_zf.at[0, d], sem_zf.at[1, d],
            device_id=(my_x * nz + peer, narrow), device_id_type=MESH,
        )

    def xf_copy(d):
        peer = x_peers[d]
        return pltpu.make_async_remote_copy(
            send_xf.at[peer], recv_xf.at[d], sem_xf.at[0, d], sem_xf.at[1, d],
            device_id=(peer * nz + my_z, narrow), device_id_type=MESH,
        )

    def zf_send(c):
        send_zf[...] = acc[c].astype(BF).reshape(send_zf.shape)
        for d in range(nz - 1):
            zf_copy(d).start()

    def zf_sum(c):
        rows = [acc[c, pl.ds(pl.multiple_of(x * x_rows + my_z * rows_dev, rows_dev), rows_dev), :] for x in range(nx)]
        for d in range(nz - 1):
            zf_copy(d).wait_recv()
        for x in range(nx):
            total = rows[x]
            for d in range(nz - 1):
                total += recv_zf[d, x].astype(F32)
            own_xf[x] = total
            send_xf[x] = total.astype(BF)
        for d in range(nx - 1):
            xf_copy(d).start()

    def xf_sum():
        total = own_xf[my_x]
        for d in range(nx - 1):
            xf_copy(d).wait_recv()
            total += recv_xf[d].astype(F32)
        return total

    def x_send(c):
        send_x[c] = acc[c].astype(BF)
        if c == last:
            for q in range(parts):
                for d in range(nx - 1):
                    sub_copy(q, d).start()
        else:
            for d in range(nx - 1):
                x_copy(c, d).start()

    def sub_sum(q):
        rows = slice(q * part_rows, (q + 1) * part_rows)
        total = acc[last, pl.ds(pl.multiple_of(my_x * x_rows + q * part_rows, part_rows), part_rows), :]
        for d in range(nx - 1):
            sub_copy(q, d).wait_recv()
            total += recv_x[last, d, rows].astype(F32)
        own_z[last, rows] = total
        send_z[last, rows] = total.astype(BF)
        for d in range(nz - 1):
            pl.when((z_peers[d] >> bits(nz // parts)) == q)(z_copy(last, d).start)

    def owner_sum(c):
        y_copy(micro - 1, c).wait_recv()
        acc[c] += nn(onehot[micro - 1], recv_y[micro - 1, c])
        x_send(c)

    def x_sum(c):
        total = acc[c, pl.ds(pl.multiple_of(my_x * x_rows, x_rows), x_rows), :]
        for d in range(nx - 1):
            x_copy(c, d).wait_recv()
            total += recv_x[c, d].astype(F32)
        own_z[c] = total
        send_z[c] = total.astype(BF)
        for d in range(nz - 1):
            z_copy(c, d).start()

    def z_sum(c):
        total = own_z[c, pl.ds(pl.multiple_of(my_z * rows_dev, rows_dev), rows_dev), :]
        for d in range(nz - 1):
            z_copy(c, d).wait_recv()
            total += recv_z[c, d].astype(F32)
        return total

    def far_copy(i):
        return pltpu.make_async_remote_copy(
            send_far.at[i], recv_far.at[i], sem_far.at[0, i], sem_far.at[1, i],
            device_id=(wide, opposite(narrow)), device_id_type=MESH,
        )

    def finish(c, total):
        out[:, c * CW : (c + 1) * CW] = total
        return jnp.sum(total * total, axis=1, keepdims=True)

    for s in range(micro):
        for g in range(2):
            for i, block in enumerate(owner_rows(s, slots // 2, lab_near.at[g])):
                onehot_near[s, g, :, i * 128 : (i + 1) * 128] = block
    for c in range(SHORT):
        for s in range(micro):
            for g, table in enumerate((c, chunks + c)):
                near_copy(s, c, g).wait_recv()
                part = nn(onehot_near[s, g], recv_near[s, c, g])
                acc[table] = part if s == 0 else acc[table] + part
        if c == 0:
            send_rows(1, SHORT)
            zf_send(chunks)
        else:
            x_send(chunks + c)
        x_send(c)
    send_rows(1, chunks - 1)
    for s in range(micro):
        for i, block in enumerate(owner_rows(s, slots, lab_recv)):
            onehot[s, :, i * 128 : (i + 1) * 128] = block
    for s in range(micro - 1):
        for c in range(SHORT, chunks):
            y_copy(s, c).wait_recv()
            part = nn(onehot[s], recv_y[s, c])
            acc[c] = part if s == 0 else acc[c] + part
    x_sum(0)
    owner_sum(2)
    x_sum(chunks + 1)
    x_sum(1)
    zf_sum(chunks)
    owner_sum(3)
    send_far[0] = xf_sum().astype(BF)
    far_copy(0).start()
    x_sum(2)
    send_far[1] = z_sum(chunks + 1).astype(BF)
    far_copy(1).start()
    for q in range(parts):
        sub_sum(q)
    squares = finish(2, z_sum(2))
    for c in range(SHORT):
        total = z_sum(c)
        far_copy(c).wait_recv()
        squares += finish(c, total + recv_far[c].astype(F32))
    squares += finish(last, z_sum(last))
    out[...] = out[...] * (clip_norm / jnp.maximum(jnp.sqrt(squares), clip_norm))
    labels_in.wait_send()
    labels_near.wait_send()
    for s in range(micro):
        for c in range(SHORT):
            for g in range(2):
                near_copy(s, c, g).wait_send()
        for c in range(SHORT, chunks):
            y_copy(s, c).wait_send()
    for c in range(SHORT):
        far_copy(c).wait_send()
    for d in range(nz - 1):
        zf_copy(d).wait_send()
    for d in range(nx - 1):
        xf_copy(d).wait_send()
        for q in range(parts):
            sub_copy(q, d).wait_send()
    for c in (0, 1, 2, 3, chunks + 1):
        if c != last:
            for d in range(nx - 1):
                x_copy(c, d).wait_send()
        for d in range(nz - 1):
            z_copy(c, d).wait_send()


def on_device(dims, tokens, cotangent, lengths, item_rows, w_in, w_out, table, moment_one, moment_two):
    nx, nz, ny, cores, rows_dev = dims
    micro, positions, width = tokens.shape
    owners = ny * cores
    cap = 2 * positions // owners
    slots = owners * cap
    owned = nx * nz * rows_dev
    x_rows = nz * rows_dev
    chunks = width // CW
    vmem = pl.BlockSpec(memory_space=pltpu.VMEM)
    hbm = pl.BlockSpec(memory_space=pl.ANY)
    dma = pltpu.SemaphoreType.DMA
    clipped = pl.pallas_call(
        functools.partial(kernel, dims),
        out_shape=jax.ShapeDtypeStruct((rows_dev, width), F32),
        in_specs=[hbm, hbm, pl.BlockSpec(memory_space=pltpu.SMEM), hbm, hbm, hbm],
        out_specs=vmem,
        scratch_shapes=[
            pltpu.VMEM(tokens.shape, BF),
            pltpu.VMEM(cotangent.shape, BF),
            pltpu.VMEM(item_rows.shape, I32),
            pltpu.VMEM(w_in.shape, BF),
            pltpu.VMEM(w_out.shape, BF),
            pltpu.VMEM((positions, 4 * width), BF),
            pltpu.VMEM((positions, 4 * width), F32),
            pltpu.VMEM((HEADS, positions, positions), BF),
            pltpu.VMEM((HEADS, positions, positions), F32),
            pltpu.VMEM((positions, width), F32),
            pltpu.VMEM((2, positions, positions), BF),
            pltpu.VMEM((positions, width), BF),
            pltpu.VMEM((positions, 4 * width), BF),
            pltpu.VMEM((3, positions // 2, positions // 2), F32),
            pltpu.VMEM((micro, slots, positions), BF),
            pltpu.VMEM((owners, micro, 128), F32),
            pltpu.VMEM((owners, micro, 128), F32),
            pltpu.VMEM((2, owners // 2, micro, 128), F32),
            pltpu.VMEM((micro, owned, slots), BF),
            pltpu.VMEM((micro, 2, owned, slots // 2), BF),
            pltpu.VMEM((micro, SHORT, 2, slots // 2, CW), BF),
            pltpu.VMEM((micro, chunks, slots, CW), BF),
            pltpu.VMEM((micro, chunks, slots, CW), BF),
            pltpu.VMEM((chunks + 2, owned, CW), F32),
            pltpu.VMEM((chunks + 2, owned, CW), BF),
            pltpu.VMEM((chunks + 2, max(nx - 1, 1), x_rows, CW), BF),
            pltpu.VMEM((chunks + 2, x_rows, CW), F32),
            pltpu.VMEM((chunks + 2, x_rows, CW), BF),
            pltpu.VMEM((chunks + 2, max(nz - 1, 1), rows_dev, CW), BF),
            pltpu.VMEM((nx, nz, rows_dev, CW), BF),
            pltpu.VMEM((max(nz - 1, 1), nx, rows_dev, CW), BF),
            pltpu.VMEM((nx, rows_dev, CW), F32),
            pltpu.VMEM((nx, rows_dev, CW), BF),
            pltpu.VMEM((max(nx - 1, 1), rows_dev, CW), BF),
            pltpu.VMEM((2, rows_dev, CW), BF),
            pltpu.VMEM((2, rows_dev, CW), BF),
            dma((6 + 2 * micro,)),
            dma((4,)),
            dma((2, micro, SHORT, 2)),
            dma((2, 2)),
            dma((2, max(nz - 1, 1))),
            dma((2, max(nx - 1, 1))),
            dma((2, min(nz, 4), max(nx - 1, 1))),
            dma((micro, chunks)),
            dma((micro, chunks)),
            dma((chunks + 2, max(nx - 1, 1))),
            dma((chunks + 2, max(nx - 1, 1))),
            dma((chunks + 2, max(nz - 1, 1))),
            dma((chunks + 2, max(nz - 1, 1))),
        ],
        compiler_params=pltpu.CompilerParams(collective_id=0, has_side_effects=True, vmem_limit_bytes=56 * 1024 * 1024),
        name="layer_rows",
    )(tokens, cotangent, lengths, item_rows, w_in, w_out)
    return adam_rows(clipped, table, moment_one, moment_two)


def solution(mesh, x_chips=X_CHIPS, cores=2, rows_dev=32):
    nx = x_chips
    nz = mesh.shape["wide"] // nx
    ny = mesh.shape["narrow"] // cores
    split = P(("wide", "narrow"))
    rows = P(("wide", "narrow"), None)
    return jax.shard_map(
        functools.partial(on_device, (nx, nz, ny, cores, rows_dev)),
        mesh=mesh,
        in_specs=(P(("wide", "narrow"), None, None), P(("wide", "narrow"), None, None), split, rows, P(), P(), rows, rows, rows),
        out_specs=(rows, rows, rows),
        check_vma=False,
    )
```

```python
import functools

import jax
import jax.numpy as jnp
from jax import lax
from jax.experimental import pallas as pl
from jax.experimental.pallas import tpu as pltpu
from jax.sharding import PartitionSpec as P

HEADS = 8
BF = jnp.bfloat16
F32 = jnp.float32
I32 = jnp.int32
MESH = pl.DeviceIdType.MESH
CW = 128
SHORT = 2
X_CHIPS = 4

norm_eps = 1e-06
clip_norm = 4.0
learn_rate = 0.5
beta_first = 0.9
beta_second = 0.999
adam_step = 3.0
adam_eps = 1e-08


def nn(a, b):
    return lax.dot_general(a, b, (((1,), (0,)), ((), ())), preferred_element_type=F32)


def nt(a, b):
    return lax.dot_general(a, b, (((1,), (1,)), ((), ())), preferred_element_type=F32)


def bits(n):
    return n.bit_length() - 1


def adam_rows(clipped, table, moment_one, moment_two):
    first_moment = beta_first * moment_one + (1.0 - beta_first) * clipped
    second_moment = beta_second * moment_two + (1.0 - beta_second) * clipped * clipped
    step_size = learn_rate / (1.0 - beta_first**adam_step)
    scaled = jnp.sqrt(second_moment / (1.0 - beta_second**adam_step)) + adam_eps
    return (table - step_size * first_moment / scaled, first_moment, second_moment)


def iota(shape, dim):
    return lax.broadcasted_iota(I32, shape, dim)


def as_one(flags):
    return jnp.where(flags, 1.0, 0.0).astype(BF)


def layout_rows(s, items, owners, cap, rows_dev, pack, lab_send):
    positions = items.shape[1]
    ids = items[pl.ds(s, 1), :]
    ids_col = jnp.transpose(jnp.broadcast_to(ids.astype(F32), (8, positions)))[:, 0:1].astype(I32)
    owner = (ids >> bits(rows_dev)) & (owners - 1)
    owner_col = (ids_col >> bits(rows_dev)) & (owners - 1)
    before = (owner_col == owner) & (iota((positions, positions), 0) < iota((positions, positions), 1))
    rank = jnp.sum(jnp.where(before, 1.0, 0.0), axis=0, keepdims=True)
    rank_col = jnp.transpose(jnp.broadcast_to(rank, (8, positions)))[:, 0:1].astype(I32)
    slot = owner * cap + rank.astype(I32)
    pack[s] = as_one(iota((owners * cap, positions), 0) == slot)
    ranks = as_one((iota((positions, 128), 1) & (cap - 1)) == rank_col)
    mine = iota((owners, positions), 0) == owner
    high = jnp.where(mine, ((ids >> bits(rows_dev * owners)) + 1).astype(F32), 0.0).astype(BF)
    low = jnp.where(mine, (ids & (rows_dev - 1)).astype(F32), 0.0).astype(BF)
    labels = (nn(high, ranks) - 1.0) * float(rows_dev) + nn(low, ranks)
    for d in range(owners):
        lab_send[d, pl.ds(s, 1), :] = labels[d : d + 1, :]


def sequence_grad(s, tokens, cot, lengths, w_in, w_out, arrived, hid, der, att, fac, mixed, ds, dmx, dinner, wmask):
    positions, width = tokens.shape[1:]
    half = positions // 2
    per_head = width // HEADS
    arrived("tokens", s)
    x = tokens[s]
    n = lengths[s]
    for part in range(4):
        cols = slice(part * width, (part + 1) * width)
        arrived("w_in", s, part)
        inner = nn(x, w_in[:, cols])
        sig = 0.5 * jnp.tanh(0.5 * inner) + 0.5
        act = inner * sig
        hid[:, cols] = act.astype(BF)
        der[:, cols] = sig + act * (1.0 - sig)
    pos = iota((positions, 1), 0)
    live = jnp.where(pos < n, 1.0, 0.0)
    weight = live / jnp.full((positions, 1), n, I32).astype(F32)
    causal = iota((half, half), 1) <= iota((half, half), 0)
    wmask[0] = jnp.where(causal, weight[:half], 0.0)
    wmask[1] = jnp.broadcast_to(weight[half:], (half, half))
    wmask[2] = jnp.where(causal, weight[half:], 0.0)
    low = iota((positions, 128), 1) < per_head
    ones = (jnp.where(iota((1, 128), 1) < per_head, 1.0, 0.0).astype(BF), jnp.where(iota((1, 128), 1) < per_head, 0.0, 1.0).astype(BF))
    scale = per_head ** (-0.5)

    def score(block, wm):
        sig = 0.5 * jnp.tanh(0.5 * block) + 0.5
        act = block * sig
        return (act * wm).astype(BF), (sig + act * (1.0 - sig)) * wm

    for pair in range(HEADS // 2):
        v2 = hid[:, width + pair * 128 : width + (pair + 1) * 128]
        q2 = hid[:, 2 * width + pair * 128 : 2 * width + (pair + 1) * 128]
        k2 = hid[:, 3 * width + pair * 128 : 3 * width + (pair + 1) * 128]
        for h in range(2):
            head = 2 * pair + h
            qm = q2 * (ones[h] * scale)
            a, f = score(nt(qm[:half], k2[:half]), wmask[0])
            att[head, :half, :half] = a
            fac[head, :half, :half] = f
            below = nt(qm[half:], k2)
            a, f = score(below[:, :half], wmask[1])
            att[head, half:, :half] = a
            fac[head, half:, :half] = f
            a, f = score(below[:, half:], wmask[2])
            att[head, half:, half:] = a
            fac[head, half:, half:] = f
        mixed[:, pair * 128 : (pair + 1) * 128] = jnp.where(low, nn(att[2 * pair], v2), nn(att[2 * pair + 1], v2))

    mix = mixed[...]
    centered = mix - jnp.mean(mix, axis=1, keepdims=True)
    inv = lax.rsqrt(jnp.mean(centered * centered, axis=1, keepdims=True) + norm_eps)
    normed = centered * inv
    arrived("cot", s)
    dgated = (nt(cot[s], w_out[...]) * live).astype(BF).astype(F32)
    gate = hid[:, :width].astype(F32)
    dgate = (dgated * normed).astype(BF).astype(F32)
    dinner[:, :width] = (dgate * der[:, :width]).astype(BF)
    dnormed = dgated * gate
    dcentered = inv * (dnormed - normed * jnp.mean(dnormed * normed, axis=1, keepdims=True))
    dmx[...] = (dcentered - jnp.mean(dcentered, axis=1, keepdims=True)).astype(BF)

    for pair in range(HEADS // 2):
        lanes = slice(pair * 128, (pair + 1) * 128)
        v_at = slice(width + pair * 128, width + (pair + 1) * 128)
        q_at = slice(2 * width + pair * 128, 2 * width + (pair + 1) * 128)
        k_at = slice(3 * width + pair * 128, 3 * width + (pair + 1) * 128)
        v2, k2 = hid[:, v_at], hid[:, k_at]
        dm2 = dmx[:, lanes]
        dm2_t = jnp.transpose(dm2)
        q2_t = jnp.transpose(hid[:, q_at])
        for h in range(2):
            head = 2 * pair + h
            dmm = dm2 * ones[h]
            d = nt(dmm[:half], v2[:half])
            ds[h, :half, :half] = (d.astype(BF).astype(F32) * fac[head, :half, :half]).astype(BF)
            d = nt(dmm[half:], v2)
            ds[h, half:, :] = (d.astype(BF).astype(F32) * fac[head, half:, :]).astype(BF)
        dv = jnp.concatenate([nn(dm2_t[:per_head], att[2 * pair]), nn(dm2_t[per_head:], att[2 * pair + 1])], axis=0)
        dk = jnp.concatenate([nn(q2_t[:per_head], ds[0]), nn(q2_t[per_head:], ds[1])], axis=0)
        dq = jnp.where(low, nn(ds[0], k2), nn(ds[1], k2))
        dinner[:, v_at] = (jnp.transpose(dv).astype(BF).astype(F32) * der[:, v_at]).astype(BF)
        dinner[:, q_at] = ((dq * scale).astype(BF).astype(F32) * der[:, q_at]).astype(BF)
        dinner[:, k_at] = ((jnp.transpose(dk) * scale).astype(BF).astype(F32) * der[:, k_at]).astype(BF)
    return live


def kernel(
    dims, tokens_hbm, cot_hbm, lengths, items_hbm, w_in_hbm, w_out_hbm, out,
    tokens, cot, items, w_in, w_out,
    hid, der, att, fac, mixed, ds, dmx, dinner, wmask, pack, lab_send, lab_recv, lab_near, onehot, onehot_near, recv_near,
    send_y, recv_y, acc, send_x, recv_x, own_z, send_z, recv_z, send_zf, recv_zf, own_xf, send_xf, recv_xf, send_far, recv_far,
    sem_in, sem_lab, sem_near, sem_far, sem_zf, sem_xf, sem_sub, sem_y_send, sem_y_recv, sem_x_send, sem_x_recv, sem_z_send, sem_z_recv,
):
    nx, nz, ny, cores, rows_dev = dims
    micro, positions, width = tokens.shape
    owners = ny * cores
    cap = 2 * positions // owners
    slots = owners * cap
    owned = nx * nz * rows_dev
    x_rows = nz * rows_dev
    chunks = width // CW
    wide, narrow = lax.axis_index("wide"), lax.axis_index("narrow")
    my_x, my_z = wide >> bits(nz), wide & (nz - 1)
    my_y, my_core = narrow >> bits(cores), narrow & (cores - 1)

    copies = {("items",): pltpu.make_async_copy(items_hbm, items, sem_in.at[0])}
    copies["tokens", 0] = pltpu.make_async_copy(tokens_hbm.at[0], tokens.at[0], sem_in.at[1])
    for part in range(4):
        cols = pl.ds(part * width, width)
        copies["w_in", part] = pltpu.make_async_copy(w_in_hbm.at[:, cols], w_in.at[:, cols], sem_in.at[2 + part])
    copies["w_out",] = pltpu.make_async_copy(w_out_hbm, w_out, sem_in.at[6])
    copies["cot", 0] = pltpu.make_async_copy(cot_hbm.at[0], cot.at[0], sem_in.at[7])
    for s in range(1, micro):
        copies["tokens", s] = pltpu.make_async_copy(tokens_hbm.at[s], tokens.at[s], sem_in.at[6 + 2 * s])
        copies["cot", s] = pltpu.make_async_copy(cot_hbm.at[s], cot.at[s], sem_in.at[7 + 2 * s])
    for copy in copies.values():
        copy.start()

    def arrived(name, s, part=0):
        @pl.when(s == 0)
        def _():
            copies[(name, part)].wait()
            if name == "cot":
                copies["w_out",].wait()

        if name != "w_in":
            for later in range(1, micro):
                pl.when(s == later)(copies[name, later].wait)

    hops = sorted(((dy, dc) for dy in range(ny) for dc in range(cores)), key=lambda h: (-min(h[0], ny - h[0]), h[1], h[0]))
    hops.remove((0, 0))
    near = [((my_y + dy) & (ny - 1)) * cores + ((my_core + dc) & (cores - 1)) for dy, dc in hops]
    quarter = ny // 4
    ahead = [0] + [sign * d for d in range(1, quarter) for sign in (1, -1)]
    if quarter:
        ahead.append(quarter - 2 * quarter * my_core)
    close = [((my_y + dy) & (ny - 1)) * cores + ((my_core + dc) & (cores - 1)) for dy in ahead for dc in range(cores)]

    def opposite(owner):
        return (owner + owners // 2) & (owners - 1)

    x_peers = [(my_x + d) & (nx - 1) for d in range(1, nx)]
    z_peers = [(my_z + d) & (nz - 1) for d in range(1, nz)]

    barrier = pltpu.get_barrier_semaphore()
    for peer in near:
        pl.semaphore_signal(barrier, inc=1, device_id=(wide, peer), device_id_type=MESH)
    for peer in x_peers:
        pl.semaphore_signal(barrier, inc=1, device_id=(peer * nz + my_z, narrow), device_id_type=MESH)
    for peer in z_peers:
        pl.semaphore_signal(barrier, inc=1, device_id=(my_x * nz + peer, narrow), device_id_type=MESH)

    half = positions // 2
    for head in range(HEADS):
        att[head, :half, half:] = jnp.zeros((half, half), BF)
    for h in range(2):
        ds[h, :half, half:] = jnp.zeros((half, half), BF)

    copies["items",].wait()
    for s in range(micro):
        layout_rows(s, items, owners, cap, rows_dev, pack, lab_send)
    lab_recv[0] = lab_send[narrow]
    lab_near[0, 0] = lab_send[narrow]
    lab_near[1, 0] = lab_send[opposite(narrow)]

    def slots_of(owner):
        return pl.ds(pl.multiple_of(owner * cap, cap), cap)

    def send_rows(s, c):
        for k, peer in enumerate(near):
            pltpu.make_async_remote_copy(
                send_y.at[s, c, slots_of(peer)], recv_y.at[s, c, pl.ds((k + 1) * cap, cap)],
                sem_y_send.at[s, c], sem_y_recv.at[s, c],
                device_id=(wide, peer), device_id_type=MESH,
            ).start()
        recv_y[s, c, :cap] = send_y[s, c, slots_of(narrow), :]

    def send_rows_near(s, c):
        for k, peer in enumerate(close):
            for g, owner in enumerate((peer, opposite(peer))):
                if k == 0:
                    recv_near[s, c, g, :cap] = send_y[s, c, slots_of(owner), :]
                else:
                    pltpu.make_async_remote_copy(
                        send_y.at[s, c, slots_of(owner)], recv_near.at[s, c, g, pl.ds(k * cap, cap)],
                        sem_near.at[0, s, c, g], sem_near.at[1, s, c, g],
                        device_id=(wide, peer), device_id_type=MESH,
                    ).start()

    def one_sequence(s, carry):
        live = sequence_grad(s, tokens, cot, lengths, w_in, w_out, arrived, hid, der, att, fac, mixed, ds, dmx, dinner, wmask)

        @pl.when(s == 0)
        def _():
            pl.semaphore_wait(barrier, len(near) + len(x_peers) + len(z_peers))
            for k, peer in enumerate(near):
                pltpu.make_async_remote_copy(
                    lab_send.at[peer], lab_recv.at[k + 1], sem_lab.at[0], sem_lab.at[1],
                    device_id=(wide, peer), device_id_type=MESH,
                ).start()
            for k, peer in enumerate(close[1:], 1):
                for g, owner in enumerate((peer, opposite(peer))):
                    pltpu.make_async_remote_copy(
                        lab_send.at[owner], lab_near.at[g, k], sem_lab.at[2], sem_lab.at[3],
                        device_id=(wide, peer), device_id_type=MESH,
                    ).start()

        for w in range(width // 256):
            cols = slice(w * 256, (w + 1) * 256)
            dx = nt(dinner[...], w_in[cols, :]).astype(BF).astype(F32)
            grad = (dx + cot[s, :, cols].astype(F32) * live).astype(BF)
            packed = nn(pack[s], grad).astype(BF)
            for c in range(w * 256 // CW, (w + 1) * 256 // CW):
                send_y[s, c] = packed[:, c * CW - w * 256 : (c + 1) * CW - w * 256]
                if c < SHORT:
                    send_rows_near(s, c)
                if c == SHORT:
                    pl.when(s < micro - 1)(functools.partial(send_rows, s, c))
        return carry

    lax.fori_loop(0, micro, one_sequence, 0)
    send_rows(0, chunks - 1)

    def whole(src, dst, send, recv):
        return pltpu.make_async_remote_copy(src, dst, send, recv, device_id=(wide, narrow), device_id_type=MESH)

    labels_in = whole(lab_send.at[pl.ds(1, owners - 1)], lab_recv.at[pl.ds(1, owners - 1)], sem_lab.at[0], sem_lab.at[1])
    near_count = 2 * (owners // 2 - 1)
    labels_near = whole(lab_send.at[pl.ds(1, near_count)], lab_recv.at[pl.ds(1, near_count)], sem_lab.at[2], sem_lab.at[3])
    labels_near.wait_recv()
    labels_in.wait_recv()
    group = 128 // cap
    lane = iota((1, 128), 1)

    def owner_rows(s, count, labels):
        blocks = []
        for g in range(count // 128):
            row = labels[g * group, s : s + 1, :]
            for k in range(1, group):
                row = jnp.where(lane >= k * cap, labels[g * group + k, s : s + 1, :], row)
            blocks.append(as_one(iota((owned, 128), 0) == row.astype(I32)))
        return blocks

    def near_copy(s, c, g):
        rest = pl.ds(cap, slots // 2 - cap)
        return whole(send_y.at[s, c, rest], recv_near.at[s, c, g, rest], sem_near.at[0, s, c, g], sem_near.at[1, s, c, g])

    def y_copy(s, c):
        return whole(send_y.at[s, c, pl.ds(cap, slots - cap)], recv_y.at[s, c, pl.ds(cap, slots - cap)], sem_y_send.at[s, c], sem_y_recv.at[s, c])

    def x_copy(c, d):
        peer = x_peers[d]
        return pltpu.make_async_remote_copy(
            send_x.at[c, pl.ds(pl.multiple_of(peer * x_rows, x_rows), x_rows)], recv_x.at[c, d],
            sem_x_send.at[c, d], sem_x_recv.at[c, d],
            device_id=(peer * nz + my_z, narrow), device_id_type=MESH,
        )

    def z_copy(c, d):
        peer = z_peers[d]
        return pltpu.make_async_remote_copy(
            send_z.at[c, pl.ds(pl.multiple_of(peer * rows_dev, rows_dev), rows_dev)], recv_z.at[c, d],
            sem_z_send.at[c, d], sem_z_recv.at[c, d],
            device_id=(my_x * nz + peer, narrow), device_id_type=MESH,
        )

    last = chunks - 1
    parts = min(nz, 4)
    part_rows = x_rows // parts

    def sub_copy(q, d):
        peer = x_peers[d]
        rows = pl.ds(pl.multiple_of(peer * x_rows + q * part_rows, part_rows), part_rows)
        return pltpu.make_async_remote_copy(
            send_x.at[last, rows], recv_x.at[last, d, pl.ds(q * part_rows, part_rows)],
            sem_sub.at[0, q, d], sem_sub.at[1, q, d],
            device_id=(peer * nz + my_z, narrow), device_id_type=MESH,
        )

    def zf_copy(d):
        peer = z_peers[d]
        return pltpu.make_async_remote_copy(
            send_zf.at[:, peer], recv_zf.at[d], sem_zf.at[0, d], sem_zf.at[1, d],
            device_id=(my_x * nz + peer, narrow), device_id_type=MESH,
        )

    def xf_copy(d):
        peer = x_peers[d]
        return pltpu.make_async_remote_copy(
            send_xf.at[peer], recv_xf.at[d], sem_xf.at[0, d], sem_xf.at[1, d],
            device_id=(peer * nz + my_z, narrow), device_id_type=MESH,
        )

    def zf_send(c):
        send_zf[...] = acc[c].astype(BF).reshape(send_zf.shape)
        for d in range(nz - 1):
            zf_copy(d).start()

    def zf_sum(c):
        rows = [acc[c, pl.ds(pl.multiple_of(x * x_rows + my_z * rows_dev, rows_dev), rows_dev), :] for x in range(nx)]
        for d in range(nz - 1):
            zf_copy(d).wait_recv()
        for x in range(nx):
            total = rows[x]
            for d in range(nz - 1):
                total += recv_zf[d, x].astype(F32)
            own_xf[x] = total
            send_xf[x] = total.astype(BF)
        for d in range(nx - 1):
            xf_copy(d).start()

    def xf_sum():
        total = own_xf[my_x]
        for d in range(nx - 1):
            xf_copy(d).wait_recv()
            total += recv_xf[d].astype(F32)
        return total

    def x_send(c):
        send_x[c] = acc[c].astype(BF)
        if c == last:
            for q in range(parts):
                for d in range(nx - 1):
                    sub_copy(q, d).start()
        else:
            for d in range(nx - 1):
                x_copy(c, d).start()

    def sub_sum(q):
        rows = slice(q * part_rows, (q + 1) * part_rows)
        total = acc[last, pl.ds(pl.multiple_of(my_x * x_rows + q * part_rows, part_rows), part_rows), :]
        for d in range(nx - 1):
            sub_copy(q, d).wait_recv()
            total += recv_x[last, d, rows].astype(F32)
        own_z[last, rows] = total
        send_z[last, rows] = total.astype(BF)
        for d in range(nz - 1):
            pl.when((z_peers[d] >> bits(nz // parts)) == q)(z_copy(last, d).start)

    def owner_sum(c):
        y_copy(micro - 1, c).wait_recv()
        acc[c] += nn(onehot[micro - 1], recv_y[micro - 1, c])
        x_send(c)

    def x_sum(c):
        total = acc[c, pl.ds(pl.multiple_of(my_x * x_rows, x_rows), x_rows), :]
        for d in range(nx - 1):
            x_copy(c, d).wait_recv()
            total += recv_x[c, d].astype(F32)
        own_z[c] = total
        send_z[c] = total.astype(BF)
        for d in range(nz - 1):
            z_copy(c, d).start()

    def z_sum(c):
        total = own_z[c, pl.ds(pl.multiple_of(my_z * rows_dev, rows_dev), rows_dev), :]
        for d in range(nz - 1):
            z_copy(c, d).wait_recv()
            total += recv_z[c, d].astype(F32)
        return total

    def far_copy(i):
        return pltpu.make_async_remote_copy(
            send_far.at[i], recv_far.at[i], sem_far.at[0, i], sem_far.at[1, i],
            device_id=(wide, opposite(narrow)), device_id_type=MESH,
        )

    def finish(c, total):
        out[:, c * CW : (c + 1) * CW] = total
        return jnp.sum(total * total, axis=1, keepdims=True)

    for s in range(micro):
        for g in range(2):
            for i, block in enumerate(owner_rows(s, slots // 2, lab_near.at[g])):
                onehot_near[s, g, :, i * 128 : (i + 1) * 128] = block
    for c in range(SHORT):
        for s in range(micro):
            for g, table in enumerate((c, chunks + c)):
                near_copy(s, c, g).wait_recv()
                part = nn(onehot_near[s, g], recv_near[s, c, g])
                acc[table] = part if s == 0 else acc[table] + part
        if c == 0:
            zf_send(chunks)
        else:
            x_send(chunks + c)
        x_send(c)
    send_rows(1, SHORT)
    for s in range(micro):
        for i, block in enumerate(owner_rows(s, slots, lab_recv)):
            onehot[s, :, i * 128 : (i + 1) * 128] = block
    for s in range(micro - 1):
        for c in range(SHORT, chunks):
            if c == last:
                send_rows(1, last)
            y_copy(s, c).wait_recv()
            part = nn(onehot[s], recv_y[s, c])
            acc[c] = part if s == 0 else acc[c] + part
    x_sum(0)
    owner_sum(2)
    x_sum(chunks + 1)
    x_sum(1)
    zf_sum(chunks)
    owner_sum(3)
    send_far[0] = xf_sum().astype(BF)
    far_copy(0).start()
    x_sum(2)
    send_far[1] = z_sum(chunks + 1).astype(BF)
    far_copy(1).start()
    for q in range(parts):
        sub_sum(q)
    squares = finish(2, z_sum(2))
    for c in range(SHORT):
        total = z_sum(c)
        far_copy(c).wait_recv()
        squares += finish(c, total + recv_far[c].astype(F32))
    squares += finish(last, z_sum(last))
    out[...] = out[...] * (clip_norm / jnp.maximum(jnp.sqrt(squares), clip_norm))
    labels_in.wait_send()
    labels_near.wait_send()
    for s in range(micro):
        for c in range(SHORT):
            for g in range(2):
                near_copy(s, c, g).wait_send()
        for c in range(SHORT, chunks):
            y_copy(s, c).wait_send()
    for c in range(SHORT):
        far_copy(c).wait_send()
    for d in range(nz - 1):
        zf_copy(d).wait_send()
    for d in range(nx - 1):
        xf_copy(d).wait_send()
        for q in range(parts):
            sub_copy(q, d).wait_send()
    for c in (0, 1, 2, 3, chunks + 1):
        if c != last:
            for d in range(nx - 1):
                x_copy(c, d).wait_send()
        for d in range(nz - 1):
            z_copy(c, d).wait_send()


def on_device(dims, tokens, cotangent, lengths, item_rows, w_in, w_out, table, moment_one, moment_two):
    nx, nz, ny, cores, rows_dev = dims
    micro, positions, width = tokens.shape
    owners = ny * cores
    cap = 2 * positions // owners
    slots = owners * cap
    owned = nx * nz * rows_dev
    x_rows = nz * rows_dev
    chunks = width // CW
    vmem = pl.BlockSpec(memory_space=pltpu.VMEM)
    hbm = pl.BlockSpec(memory_space=pl.ANY)
    dma = pltpu.SemaphoreType.DMA
    clipped = pl.pallas_call(
        functools.partial(kernel, dims),
        out_shape=jax.ShapeDtypeStruct((rows_dev, width), F32),
        in_specs=[hbm, hbm, pl.BlockSpec(memory_space=pltpu.SMEM), hbm, hbm, hbm],
        out_specs=vmem,
        scratch_shapes=[
            pltpu.VMEM(tokens.shape, BF),
            pltpu.VMEM(cotangent.shape, BF),
            pltpu.VMEM(item_rows.shape, I32),
            pltpu.VMEM(w_in.shape, BF),
            pltpu.VMEM(w_out.shape, BF),
            pltpu.VMEM((positions, 4 * width), BF),
            pltpu.VMEM((positions, 4 * width), F32),
            pltpu.VMEM((HEADS, positions, positions), BF),
            pltpu.VMEM((HEADS, positions, positions), F32),
            pltpu.VMEM((positions, width), F32),
            pltpu.VMEM((2, positions, positions), BF),
            pltpu.VMEM((positions, width), BF),
            pltpu.VMEM((positions, 4 * width), BF),
            pltpu.VMEM((3, positions // 2, positions // 2), F32),
            pltpu.VMEM((micro, slots, positions), BF),
            pltpu.VMEM((owners, micro, 128), F32),
            pltpu.VMEM((owners, micro, 128), F32),
            pltpu.VMEM((2, owners // 2, micro, 128), F32),
            pltpu.VMEM((micro, owned, slots), BF),
            pltpu.VMEM((micro, 2, owned, slots // 2), BF),
            pltpu.VMEM((micro, SHORT, 2, slots // 2, CW), BF),
            pltpu.VMEM((micro, chunks, slots, CW), BF),
            pltpu.VMEM((micro, chunks, slots, CW), BF),
            pltpu.VMEM((chunks + 2, owned, CW), F32),
            pltpu.VMEM((chunks + 2, owned, CW), BF),
            pltpu.VMEM((chunks + 2, max(nx - 1, 1), x_rows, CW), BF),
            pltpu.VMEM((chunks + 2, x_rows, CW), F32),
            pltpu.VMEM((chunks + 2, x_rows, CW), BF),
            pltpu.VMEM((chunks + 2, max(nz - 1, 1), rows_dev, CW), BF),
            pltpu.VMEM((nx, nz, rows_dev, CW), BF),
            pltpu.VMEM((max(nz - 1, 1), nx, rows_dev, CW), BF),
            pltpu.VMEM((nx, rows_dev, CW), F32),
            pltpu.VMEM((nx, rows_dev, CW), BF),
            pltpu.VMEM((max(nx - 1, 1), rows_dev, CW), BF),
            pltpu.VMEM((2, rows_dev, CW), BF),
            pltpu.VMEM((2, rows_dev, CW), BF),
            dma((6 + 2 * micro,)),
            dma((4,)),
            dma((2, micro, SHORT, 2)),
            dma((2, 2)),
            dma((2, max(nz - 1, 1))),
            dma((2, max(nx - 1, 1))),
            dma((2, min(nz, 4), max(nx - 1, 1))),
            dma((micro, chunks)),
            dma((micro, chunks)),
            dma((chunks + 2, max(nx - 1, 1))),
            dma((chunks + 2, max(nx - 1, 1))),
            dma((chunks + 2, max(nz - 1, 1))),
            dma((chunks + 2, max(nz - 1, 1))),
        ],
        compiler_params=pltpu.CompilerParams(collective_id=0, has_side_effects=True, vmem_limit_bytes=55040 * 1024),
        name="layer_rows",
    )(tokens, cotangent, lengths, item_rows, w_in, w_out)
    return adam_rows(clipped, table, moment_one, moment_two)


def solution(mesh, x_chips=X_CHIPS, cores=2, rows_dev=32):
    nx = x_chips
    nz = mesh.shape["wide"] // nx
    ny = mesh.shape["narrow"] // cores
    split = P(("wide", "narrow"))
    rows = P(("wide", "narrow"), None)
    return jax.shard_map(
        functools.partial(on_device, (nx, nz, ny, cores, rows_dev)),
        mesh=mesh,
        in_specs=(P(("wide", "narrow"), None, None), P(("wide", "narrow"), None, None), split, rows, P(), P(), rows, rows, rows),
        out_specs=(rows, rows, rows),
        check_vma=False,
    )
```
